256 devices in a mesh: mon: 64 (over y, z, core), out: 4 (over x).
Axes of the slice: x: 4, y: 4, z: 8, core: 2. Of those that a mesh axis runs over, the one named last changes fastest.
Arguments:
- mon_flow: bfloat16 [24576, 128], P('mon'), may hold values from -2.5 to 2.5
- out_flow: bfloat16 [4, 4096, 128], P('out', 'mon'), may hold values from -2.5 to 2.5
- rating: float32 [24576], P('mon'), may hold values from 1 to 3
- weights: float32 [128], replicated, may hold values from 0.25 to 1
- lodf: bfloat16 [64, 4, 8, 128, 128], P('mon', 'out'), may hold values from -1 to 1
- tile_mon: int32 [64, 4, 8], P('mon', 'out'), may hold values from 0 to 2
- tile_out: int32 [64, 4, 8], P('mon', 'out'), may hold values from 0 to 31
- tile_count: int32 [64, 4], P('mon', 'out'), may hold values from 1 to 8, as said below
Outputs:
- grad_mon: float32 [24576, 128], P(('mon', 'out'))
- grad_out: float32 [4, 4096, 128], P('out', 'mon')
The draws below stay inside these ranges and needn't reach their ends.
Inputs may be any that keep to these rules, and one draw needn't show every extreme that they name: `tile_count`: each device has 1 to 8 live slots; some device has exactly 8 in every draw.
All inputs are finite; a program needn't handle non-finite values.
Results may differ from the reference program's by a relative error of at most 0.00085.
Values may be sent and summed in bfloat16 or wider, within the bound.
A program may use at most 64 MiB of HBM per device.

```python
import math
import jax
import jax.numpy as jnp
from jax import lax

BLK = 128
S = 128
MB_DEV = 3
KB_DEV = 32
SLOTS = 8
M = 24576
KDEV = 4096
N_MON = 64
N_OUT = 4


def draw_tile_count(key, part):
    first = jax.random.fold_in(key, 11)
    second = jax.random.fold_in(key, 12)
    third = jax.random.fold_in(key, 13)
    base = jax.random.randint(first, (N_MON, N_OUT), 1, SLOTS // 2 + 1)
    heavy = jax.random.randint(second, (N_MON, N_OUT), 0, 8) == 0
    chosen = jax.random.randint(third, (), 0, N_MON * N_OUT)
    flat_ids = jnp.arange(N_MON * N_OUT, dtype=jnp.int32).reshape(N_MON, N_OUT)
    heavy = jnp.logical_or(heavy, flat_ids == chosen)
    return jnp.where(heavy, SLOTS, base).astype(jnp.int32)


def with_ends(entries, stream_key, smallest, top_value):
    place = [jax.random.randint(jax.random.fold_in(stream_key, axis), (), 0, length) for axis, length in enumerate(entries.shape)]
    widest = entries.shape.index(max(entries.shape))
    beside = place[:widest] + [(place[widest] + 1) % entries.shape[widest]] + place[widest + 1:]
    return entries.at[tuple(place)].set(smallest).at[tuple(beside)].set(top_value)


def block_scale(own_key, shape, shards, low, top_value):
    loudness = 1.0
    for dim, shards_of in shards:
        heights = jax.random.uniform(jax.random.fold_in(jax.random.fold_in(own_key, 6), dim), (shards_of,), jnp.float32, low / len(shards), top_value / len(shards))
        loudness = loudness * jnp.repeat(jnp.exp(heights), shape[dim] // shards_of).reshape((-1,) + (1,) * (len(shape) - 1 - dim))
    return loudness


def scatter_about(key, dims, spread, limit, shards=(), kind=jnp.bfloat16):
    level = block_scale(key, dims, shards, -0.22, 0.18) if shards else 1.0
    entries = jax.random.normal(key, dims, jnp.float32) * spread * level
    return jnp.minimum(jnp.maximum(entries, -limit), limit).astype(kind)


def setup_inputs(seed: int = 0) -> dict:
    key_of = jax.random.split(jax.random.key(seed), 9)
    mon_flow = scatter_about(key_of[0], (M, S), 0.5, 2.5, ((0, 64),))
    out_flow = scatter_about(key_of[1], (N_OUT, KDEV, S), 0.5, 2.5, ((0, 4), (1, 64)))
    rating = jnp.clip(jnp.exp(math.log(3.0) - 1.0986123 * jax.random.uniform(key_of[2], (M,), jnp.float32) ** block_scale(key_of[2], (M,), ((0, 64),), -0.2, 0.2)), 1.0, 3.0)
    weights = jnp.clip(jnp.exp(jax.random.uniform(key_of[3], (S,), jnp.float32, math.log(0.25), math.log(1.0))), 0.25, 1.0)
    lodf = scatter_about(key_of[4], (N_MON, N_OUT, SLOTS, BLK, BLK), 0.25, 1.0, ((0, 64), (1, 4)))
    tile_mon = with_ends(jax.random.randint(key_of[5], (N_MON, N_OUT, SLOTS), 0, MB_DEV), jax.random.fold_in(key_of[5], 1), 0, MB_DEV - 1).astype(jnp.int32)
    tile_out = with_ends(jax.random.randint(key_of[6], (N_MON, N_OUT, SLOTS), 0, KB_DEV), jax.random.fold_in(key_of[6], 1), 0, KB_DEV - 1).astype(jnp.int32)
    tile_count = draw_tile_count(jax.random.fold_in(key_of[8], 71), 0)
    return dict(mon_flow=mon_flow, out_flow=out_flow, rating=rating, weights=weights, lodf=lodf, tile_mon=tile_mon, tile_out=tile_out, tile_count=tile_count)


def tile_grads(lodf_tile, mon_block, out_block, rating_rows, weights):
    coupling = lodf_tile.astype(jnp.float32)
    post_flow = mon_block.astype(jnp.float32)[:, None, :] + coupling[:, :, None] * out_block.astype(jnp.float32)[None, :, :]
    inverse = 1.0 / (rating_rows * rating_rows)
    excess = post_flow * post_flow * inverse[:, None, None] - 1.0
    derivative = jax.nn.softplus(excess) * jax.nn.sigmoid(excess) * post_flow
    derivative = derivative * (4.0 / coupling.shape[0]) * inverse[:, None, None] * weights[None, None, :]
    return jnp.sum(derivative, axis=1), jnp.sum(coupling[:, :, None] * derivative, axis=0)


def reference(mon_flow, out_flow, rating, weights, lodf, tile_mon, tile_out, tile_count):
    width = lodf.shape[-1]
    scen = mon_flow.shape[1]
    mon_total = jnp.zeros(mon_flow.shape, jnp.float32)
    out_total = jnp.zeros(out_flow.shape, jnp.float32)

    def visit(totals, flat_index):
        mon_dev = flat_index // (N_OUT * SLOTS)
        remainder = flat_index % (N_OUT * SLOTS)
        out_dev = remainder // SLOTS
        slot_index = remainder % SLOTS
        live = slot_index < tile_count[mon_dev, out_dev]

        def work(inner):
            mon_part, out_part = inner
            start = ((mon_dev * MB_DEV + tile_mon[mon_dev, out_dev, slot_index]) * width).astype(jnp.int32)
            out_start = (tile_out[mon_dev, out_dev, slot_index] * width).astype(jnp.int32)
            mon_rows = lax.dynamic_slice_in_dim(mon_flow, start, width, 0)
            rating_rows = lax.dynamic_slice_in_dim(rating, start, width, 0)
            out_rows = lax.dynamic_slice(out_flow, (out_dev.astype(jnp.int32), out_start, jnp.int32(0)), (1, width, scen))[0]
            grad_m, grad_k = tile_grads(lodf[mon_dev, out_dev, slot_index], mon_rows, out_rows, rating_rows, weights)
            old_m = lax.dynamic_slice_in_dim(mon_part, start, width, 0)
            mon_part = lax.dynamic_update_slice_in_dim(mon_part, old_m + grad_m, start, 0)
            corner = (out_dev.astype(jnp.int32), out_start, jnp.int32(0))
            old_k = lax.dynamic_slice(out_part, corner, (1, width, scen))
            out_part = lax.dynamic_update_slice(out_part, old_k + grad_k[None], corner)
            return (mon_part, out_part)

        def skip(inner):
            return inner

        return lax.cond(live, work, skip, totals), None

    totals, unused = lax.scan(visit, (mon_total, out_total), jnp.arange(N_MON * N_OUT * SLOTS, dtype=jnp.int32))
    return totals[0], totals[1]
```

```python
import functools
import math

import jax
import jax.numpy as jnp
from jax import lax
from jax.experimental import pallas as pl
from jax.experimental.pallas import tpu as pltpu
from jax.sharding import PartitionSpec as P

MESH = pl.DeviceIdType.MESH
NX, NY, NZ, NC = 4, 4, 8, 2
G = NX * NC
BLK = 128
S = 128
SLOTS = 8
KC = BLK // G
ROWS = BLK // NC // G
MB = 3
OWN = MB * BLK // NX
LOG2E = math.log2(math.e)
F32 = jnp.float32
BF16 = jnp.bfloat16


def position():
    i = lax.axis_index("mon")
    o = lax.axis_index("out")
    c = lax.rem(i, NC)
    z = lax.rem(i // NC, NZ)
    y = i // (NC * NZ)
    return o, y, z, c


def at(o, y, z, c):
    return ((y * NZ + z) * NC + c, o)


def peers(o, y, z, c):
    g = o * NC + c
    group = []
    for d in range(1, G):
        other = lax.rem(g + d, G)
        group.append((other, at(other // NC, y, z, lax.rem(other, NC))))
    along_z = []
    for d in range(1, NZ):
        other = lax.rem(z + d, NZ)
        along_z.append((other, at(o, y, other, c)))
    along_y = []
    for d in range(1, NY):
        other = lax.rem(y + d, NY)
        along_y.append((other, at(o, other, z, c)))
    return g, group, along_z, along_y


def signal_all(devices):
    barrier = pltpu.get_barrier_semaphore()
    for device in devices:
        pl.semaphore_signal(barrier, inc=1, device_id=device, device_id_type=MESH)


def send(src, dst, send_sem, recv_sem, device):
    copy = pltpu.make_async_remote_copy(
        src_ref=src, dst_ref=dst, send_sem=send_sem, recv_sem=recv_sem, device_id=device, device_id_type=MESH
    )
    copy.start()
    return copy


def gather_kernel(
    lodf_ref, flow_ref, rating_ref, mon_ref, meta_ref,
    tiles_ref, gathered_ref, mon_all_ref, small_ref, meta_all_ref,
    tiles_out, small_out, gs, gr, ms, mr, zs, zr, ys, yr,
):
    o, y, z, c = position()
    g, group, along_z, along_y = peers(o, y, z, c)
    signal_all([device for _, device in group + along_z + along_y])

    flow = flow_ref[...].astype(F32)
    small_out[...] = jnp.zeros_like(small_out)
    for m in range(G):
        small_out[m, 0:ROWS, :] = flow[m * ROWS : (m + 1) * ROWS, :]
        small_out[m, ROWS : ROWS + MB, :] = rating_ref[...]
    for q in range(SLOTS):
        turned = jnp.transpose(lodf_ref[q].astype(F32))
        for m in range(G):
            low = turned[m * ROWS : (m + 1) * ROWS, :]
            high = turned[BLK // 2 + m * ROWS : BLK // 2 + (m + 1) * ROWS, :]
            tiles_out[m, q] = jnp.concatenate([low, high], axis=0).astype(BF16)
    small_ref[g] = small_out[g]
    tiles_ref[g] = tiles_out[g]
    meta_all_ref[g] = meta_ref[...]
    mon_all_ref[c] = mon_ref[...]

    pl.semaphore_wait(pltpu.get_barrier_semaphore(), len(group) + len(along_z) + len(along_y))
    first = []
    rest = []
    for d, (other, device) in enumerate(group):
        first.append(send(small_out.at[other], small_ref.at[g], gs.at[0, d], gr.at[0, d], device))
    for d, (other, device) in enumerate(group):
        rest.append(send(meta_ref, meta_all_ref.at[g], gs.at[1, d], gr.at[1, d], device))
        rest.append(send(tiles_out.at[other], tiles_ref.at[g], gs.at[2, d], gr.at[2, d], device))
    rest.append(send(mon_ref, mon_all_ref.at[c], ms, mr, at(o, y, z, 1 - c)))
    for copy in first:
        copy.wait()
    block = jnp.concatenate([small_ref[m, 0:ROWS, :] for m in range(G)], axis=0).astype(BF16)
    mine = y * NZ + z
    gathered_ref[mine] = block
    hops = [
        send(gathered_ref.at[mine], gathered_ref.at[mine], zs.at[d], zr.at[d], device)
        for d, (_, device) in enumerate(along_z)
    ]
    for copy in hops:
        copy.wait()
    row = pl.ds(y * NZ, NZ)
    hops = [
        send(gathered_ref.at[row], gathered_ref.at[row], ys.at[d], yr.at[d], device)
        for d, (_, device) in enumerate(along_y)
    ]
    for copy in rest + hops:
        copy.wait()


def tile_kernel(
    meta_ref, tiles_ref, flow_ref, mon_ref, small_ref, weights_ref,
    grad_mon_ref, grad_out_ref,
    order, scaled, column, row_scale, spread, wide_a, wide_b, flow_rows,
):
    for c in range(NC):
        for t in range(MB):
            scale = math.sqrt(LOG2E) / small_ref[c, ROWS + t : ROWS + t + 1, :]
            row_scale[c * MB + t, :, :] = scale
            turned = jnp.transpose(jnp.broadcast_to(scale, (BLK, BLK)))
            column[pl.ds((c * MB + t) * BLK, BLK), :] = turned
            scaled[pl.ds((c * MB + t) * BLK, BLK), :] = turned * mon_ref[c, pl.ds(t * BLK, BLK), :].astype(F32)
    grad_mon_ref[...] = jnp.zeros_like(grad_mon_ref)
    grad_out_ref[...] = jnp.zeros_like(grad_out_ref)
    term = lax.broadcasted_iota(jnp.int32, spread.shape, 0)
    lane = lax.broadcasted_iota(jnp.int32, spread.shape, 1)
    spread[...] = jnp.where(lax.rem(term, KC) == lane // S, 1.0, 0.0).astype(BF16)

    def list_member(member, total):
        count = meta_ref[member, 0, 2 * SLOTS]

        def add(q, _):
            order[total + q] = member * SLOTS + q
            return 0

        lax.fori_loop(0, count, add, 0)
        return total + count

    total = lax.fori_loop(0, G, list_member, 0)

    def where_of(n):
        entry = order[jnp.minimum(n, total - 1)]
        member = entry // SLOTS
        return member, lax.rem(entry, SLOTS)

    def expand(n, wide):
        member, q = where_of(n)
        block = lax.rem(member, NC) * MB + meta_ref[member, 0, q]
        piece = tiles_ref[member, q].astype(F32) * row_scale[block]
        high = piece.astype(BF16)
        low = (piece - high.astype(F32)).astype(BF16)
        both = jnp.concatenate([high, low], axis=0)
        wide[...] = lax.dot_general(both, spread[...], (((0,), (0,)), ((), ())), preferred_element_type=F32)

    def work(n, wide, rows_at):
        member, q = where_of(n)
        block = lax.rem(member, NC) * MB + meta_ref[member, 0, q]
        outage = meta_ref[member, 0, SLOTS + q]
        start = pl.multiple_of(block * BLK, BLK)
        own = pl.ds(pl.multiple_of((member // NC) * KC, KC), KC)
        flow_rows[rows_at] = flow_ref[outage, own, :].astype(F32)
        for half in range(KC // 8):
            flows = [flow_rows[rows_at, pl.ds(half * 8 + j, 8, stride=0), :] for j in range(8)]
            sums = [None] * 8
            for i in range(BLK // 8):
                base = scaled[pl.ds(start + i * 8, 8), :]
                total_m = None
                for j in range(8):
                    factor = wide[pl.ds(i * 8, 8), pl.ds((half * 8 + j) * S, S)]
                    post = base + factor * flows[j]
                    square = post * post
                    level = jnp.log2(jnp.exp2(square) + math.e)
                    slope = (level - LOG2E) * jnp.exp2(square - level) * post
                    total_m = slope if total_m is None else total_m + slope
                    part = factor * slope
                    sums[j] = part if sums[j] is None else sums[j] + part
                grad_mon_ref[pl.ds(start + i * 8, 8), :] += total_m
            rows = jnp.concatenate([jnp.sum(v, axis=0, keepdims=True) for v in sums], axis=0)
            place = pl.ds(pl.multiple_of((member // NC) * KC + half * 8, 8), 8)
            grad_out_ref[outage, place, :] += rows

    expand(0, wide_a)

    def pair(p, _):
        expand(2 * p + 1, wide_b)
        work(2 * p, wide_a, 0)

        @pl.when(2 * p + 1 < total)
        def _():
            expand(2 * p + 2, wide_a)
            work(2 * p + 1, wide_b, 1)

        return 0

    lax.fori_loop(0, (total + 1) // 2, pair, 0)
    weight = weights_ref[...] * (4.0 / BLK * math.log(2.0) ** 2)
    grad_mon_ref[...] = grad_mon_ref[...] * column[...] * weight
    grad_out_ref[...] = grad_out_ref[...] * weight[None]


def scatter_kernel(
    mon_ref, flow_ref, grad_mon_ref, grad_out_ref,
    mon_in, y_in, y_sum, z_in, z_sum, last_in,
    gs, gr, fs, fr, zs, zr, ys, yr,
):
    o, y, z, c = position()
    g, group, along_z, along_y = peers(o, y, z, c)
    signal_all([device for _, device in group + along_z + along_y])
    pl.semaphore_wait(pltpu.get_barrier_semaphore(), len(group) + len(along_z) + len(along_y))

    hops_y = [
        send(flow_ref.at[pl.ds(other * NZ, NZ)], y_in.at[d], ys.at[d], yr.at[d], device)
        for d, (other, device) in enumerate(along_y)
    ]
    group_hops = []
    for d, (other, device) in enumerate(group):
        rows = pl.ds(pl.multiple_of(lax.rem(other, NC) * MB * BLK + (other // NC) * OWN, 8), OWN)
        group_hops.append(send(mon_ref.at[rows], mon_in.at[d], gs.at[d], gr.at[d], device))
    for copy in hops_y:
        copy.wait()
    y_sum[...] = (flow_ref[pl.ds(y * NZ, NZ)] + y_in[0]) + (y_in[1] + y_in[2])
    hops = [
        send(y_sum.at[other], z_in.at[d], zs.at[d], zr.at[d], device)
        for d, (other, device) in enumerate(along_z)
    ]
    for copy in group_hops:
        copy.wait()
    rows = pl.ds(pl.multiple_of(c * MB * BLK + o * OWN, 8), OWN)
    total = mon_ref[rows, :]
    for d in range(G - 1):
        total = total + mon_in[d]
    grad_mon_ref[...] = total
    for copy in hops:
        copy.wait()
    total = y_sum[z]
    for d in range(NZ - 1):
        total = total + z_in[d]
    for m in range(G):
        z_sum[m] = total[m * ROWS : (m + 1) * ROWS, :]
    last_in[g] = z_sum[g]
    hops = [
        send(z_sum.at[other], last_in.at[g], fs.at[d], fr.at[d], device)
        for d, (other, device) in enumerate(group)
    ]
    for copy in hops:
        copy.wait()
    for m in range(G):
        grad_out_ref[pl.ds(m * ROWS, ROWS), :] = last_in[m]


def vmem(count):
    return [pl.BlockSpec(memory_space=pltpu.VMEM)] * count


DMA = pltpu.SemaphoreType.DMA


def local(mon_flow, out_flow, rating, weights, lodf, tile_mon, tile_out, tile_count):
    blocks = NY * NZ
    meta = jnp.concatenate(
        [tile_mon[0], tile_out[0], tile_count, jnp.zeros((1, S - 2 * SLOTS - 1), jnp.int32)], axis=1
    )
    tiles, gathered, mon_all, small, meta_all = pl.pallas_call(
        gather_kernel,
        out_shape=(
            jax.ShapeDtypeStruct((G, SLOTS, KC, BLK), BF16),
            jax.ShapeDtypeStruct((blocks, G * ROWS, S), BF16),
            jax.ShapeDtypeStruct((NC, MB * BLK, S), BF16),
            jax.ShapeDtypeStruct((G, 2 * ROWS, S), F32),
            jax.ShapeDtypeStruct((G, 1, S), jnp.int32),
        ),
        in_specs=vmem(5),
        out_specs=tuple(vmem(5)),
        scratch_shapes=[
            pltpu.VMEM((G, SLOTS, KC, BLK), BF16),
            pltpu.VMEM((G, 2 * ROWS, S), F32),
            DMA((3, G - 1)), DMA((3, G - 1)), DMA, DMA,
            DMA((NZ - 1,)), DMA((NZ - 1,)), DMA((NY - 1,)), DMA((NY - 1,)),
        ],
        compiler_params=pltpu.CompilerParams(collective_id=0, has_side_effects=True),
        name="gather",
    )(lodf[0, 0], out_flow[0], rating.reshape(MB, BLK), mon_flow, meta)

    part_mon, part_out = pl.pallas_call(
        tile_kernel,
        out_shape=(
            jax.ShapeDtypeStruct((NC * MB * BLK, S), F32),
            jax.ShapeDtypeStruct((blocks, G * ROWS, S), F32),
        ),
        in_specs=[pl.BlockSpec(memory_space=pltpu.SMEM)] + vmem(5),
        out_specs=tuple(vmem(2)),
        scratch_shapes=[
            pltpu.SMEM((G * SLOTS,), jnp.int32),
            pltpu.VMEM((NC * MB * BLK, S), F32),
            pltpu.VMEM((NC * MB * BLK, S), F32),
            pltpu.VMEM((NC * MB, 1, BLK), F32),
            pltpu.VMEM((2 * KC, KC * S), BF16),
            pltpu.VMEM((BLK, KC * S), F32),
            pltpu.VMEM((BLK, KC * S), F32),
            pltpu.VMEM((2, KC, S), F32),
        ],
        compiler_params=pltpu.CompilerParams(vmem_limit_bytes=24 << 20),
        name="tiles",
    )(meta_all, tiles, gathered, mon_all, small, weights.reshape(1, S))

    grad_mon, grad_out = pl.pallas_call(
        scatter_kernel,
        out_shape=(
            jax.ShapeDtypeStruct((OWN, S), F32),
            jax.ShapeDtypeStruct((G * ROWS, S), F32),
        ),
        in_specs=vmem(2),
        out_specs=tuple(vmem(2)),
        scratch_shapes=[
            pltpu.VMEM((G - 1, OWN, S), F32),
            pltpu.VMEM((NY - 1, NZ, G * ROWS, S), F32),
            pltpu.VMEM((NZ, G * ROWS, S), F32),
            pltpu.VMEM((NZ - 1, G * ROWS, S), F32),
            pltpu.VMEM((G, ROWS, S), F32),
            pltpu.VMEM((G, ROWS, S), F32),
            DMA((G - 1,)), DMA((G - 1,)), DMA((G - 1,)), DMA((G - 1,)),
            DMA((NZ - 1,)), DMA((NZ - 1,)), DMA((NY - 1,)), DMA((NY - 1,)),
        ],
        compiler_params=pltpu.CompilerParams(
            collective_id=1, has_side_effects=True, vmem_limit_bytes=24 << 20
        ),
        name="scatter",
    )(part_mon, part_out)
    return grad_mon, grad_out[None]


def solution(mesh):
    in_specs = (
        P("mon", None),
        P("out", "mon", None),
        P("mon"),
        P(),
        P("mon", "out", None, None, None),
        P("mon", "out", None),
        P("mon", "out", None),
        P("mon", "out"),
    )
    out_specs = (P(("mon", "out"), None), P("out", "mon", None))
    return jax.shard_map(local, mesh=mesh, in_specs=in_specs, out_specs=out_specs, check_vma=False)
```

```python
import functools
import math

import jax
import jax.numpy as jnp
from jax import lax
from jax.experimental import pallas as pl
from jax.experimental.pallas import tpu as pltpu
from jax.sharding import PartitionSpec as P

MESH = pl.DeviceIdType.MESH
NX, NY, NZ, NC = 4, 4, 8, 2
G = NX * NC
BLK = 128
S = 128
SLOTS = 8
KC = BLK // G
ROWS = BLK // NC // G
MB = 3
OWN = MB * BLK // NX
LOG2E = math.log2(math.e)
VMEM_BYTES = 56 << 20
F32 = jnp.float32
BF16 = jnp.bfloat16


def position():
    i = lax.axis_index("mon")
    o = lax.axis_index("out")
    c = lax.rem(i, NC)
    z = lax.rem(i // NC, NZ)
    y = i // (NC * NZ)
    return o, y, z, c


def at(o, y, z, c):
    return ((y * NZ + z) * NC + c, o)


def peers(o, y, z, c):
    g = o * NC + c
    group = []
    for d in range(1, G):
        other = lax.rem(g + d, G)
        group.append((other, at(other // NC, y, z, lax.rem(other, NC))))
    along_z = []
    for d in range(1, NZ):
        other = lax.rem(z + d, NZ)
        along_z.append((other, at(o, y, other, c)))
    along_y = []
    for d in (1, NY - 1):
        other = lax.rem(y + d, NY)
        along_y.append((other, at(o, other, z, c)))
    return g, group, along_z, along_y


def signal_all(devices):
    barrier = pltpu.get_barrier_semaphore()
    for device in devices:
        pl.semaphore_signal(barrier, inc=1, device_id=device, device_id_type=MESH)


def send(src, dst, send_sem, recv_sem, device):
    copy = pltpu.make_async_remote_copy(
        src_ref=src, dst_ref=dst, send_sem=send_sem, recv_sem=recv_sem, device_id=device, device_id_type=MESH
    )
    copy.start()
    return copy


def gather_kernel(
    lodf_ref, flow_ref, rating_ref, mon_ref, meta_ref,
    tiles_ref, gathered_ref, mon_all_ref, small_ref, meta_all_ref,
    tiles_out, small_out, gs, gr, ms, mr, zs, zr, ys, yr,
):
    o, y, z, c = position()
    g, group, along_z, along_y = peers(o, y, z, c)
    signal_all([device for _, device in group + along_z + along_y])

    flow = flow_ref[...].astype(F32)
    small_out[...] = jnp.zeros_like(small_out)
    for m in range(G):
        small_out[m, 0:ROWS, :] = flow[m * ROWS : (m + 1) * ROWS, :]
        small_out[m, ROWS : ROWS + MB, :] = rating_ref[...]
    for q in range(SLOTS):
        turned = jnp.transpose(lodf_ref[q].astype(F32))
        for m in range(G):
            low = turned[m * ROWS : (m + 1) * ROWS, :]
            high = turned[BLK // 2 + m * ROWS : BLK // 2 + (m + 1) * ROWS, :]
            tiles_out[m, q] = jnp.concatenate([low, high], axis=0).astype(BF16)
    small_ref[g] = small_out[g]
    tiles_ref[g] = tiles_out[g]
    meta_all_ref[g] = meta_ref[...]
    mon_all_ref[c] = mon_ref[...]

    pl.semaphore_wait(pltpu.get_barrier_semaphore(), len(group) + len(along_z) + len(along_y))
    first = []
    rest = []
    for d, (other, device) in enumerate(group):
        first.append(send(small_out.at[other], small_ref.at[g], gs.at[0, d], gr.at[0, d], device))
    for d, (other, device) in enumerate(group):
        rest.append(send(meta_ref, meta_all_ref.at[g], gs.at[1, d], gr.at[1, d], device))
        rest.append(send(tiles_out.at[other], tiles_ref.at[g], gs.at[2, d], gr.at[2, d], device))
    rest.append(send(mon_ref, mon_all_ref.at[c], ms, mr, at(o, y, z, 1 - c)))
    for copy in first:
        copy.wait()
    block = jnp.concatenate([small_ref[m, 0:ROWS, :] for m in range(G)], axis=0).astype(BF16)
    mine = y * NZ + z
    gathered_ref[mine] = block
    hops = [
        send(gathered_ref.at[mine], gathered_ref.at[mine], zs.at[d], zr.at[d], device)
        for d, (_, device) in enumerate(along_z)
    ]
    for copy in hops:
        copy.wait()
    up, down = at(o, lax.rem(y + 1, NY), z, c), at(o, lax.rem(y + NY - 1, NY), z, c)

    def half(row, part):
        return gathered_ref.at[pl.ds(lax.rem(row, NY) * NZ + part * (NZ // 2), NZ // 2)]

    hops = []
    for part in range(2):
        own = half(y, part)
        hops.append(send(own, own, ys.at[0, part], yr.at[0, part], up))
        own = half(y, 1 - part)
        hops.append(send(own, own, ys.at[1, part], yr.at[1, part], down))
    hops[0].wait()
    passed = half(y + NY - 1, 0)
    hops.append(send(passed, passed, ys.at[0, 2], yr.at[0, 2], up))
    hops[1].wait()
    passed = half(y + 1, 1)
    hops.append(send(passed, passed, ys.at[1, 2], yr.at[1, 2], down))
    for copy in rest + hops[2:]:
        copy.wait()


def tile_kernel(
    meta_ref, tiles_ref, flow_ref, mon_ref, small_ref, weights_ref,
    grad_mon_ref, grad_out_ref,
    order, scaled, column, row_scale, spread, wide_a, wide_b, flow_rows,
):
    for c in range(NC):
        for t in range(MB):
            scale = math.sqrt(LOG2E) / small_ref[c, ROWS + t : ROWS + t + 1, :]
            row_scale[c * MB + t, :, :] = scale
            turned = jnp.transpose(jnp.broadcast_to(scale, (BLK, BLK)))
            column[pl.ds((c * MB + t) * BLK, BLK), :] = turned
            scaled[pl.ds((c * MB + t) * BLK, BLK), :] = turned * mon_ref[c, pl.ds(t * BLK, BLK), :].astype(F32)
    grad_mon_ref[...] = jnp.zeros_like(grad_mon_ref)
    grad_out_ref[...] = jnp.zeros_like(grad_out_ref)
    term = lax.broadcasted_iota(jnp.int32, spread.shape, 0)
    lane = lax.broadcasted_iota(jnp.int32, spread.shape, 1)
    spread[...] = jnp.where(lax.rem(term, KC) == lane // S, 1.0, 0.0).astype(BF16)

    def list_member(member, total):
        count = meta_ref[member, 0, 2 * SLOTS]

        def add(q, _):
            order[total + q] = member * SLOTS + q
            return 0

        lax.fori_loop(0, count, add, 0)
        return total + count

    total = lax.fori_loop(0, G, list_member, 0)

    def where_of(n):
        entry = order[jnp.minimum(n, total - 1)]
        member = entry // SLOTS
        return member, lax.rem(entry, SLOTS)

    def expand(n, wide):
        member, q = where_of(n)
        block = lax.rem(member, NC) * MB + meta_ref[member, 0, q]
        piece = tiles_ref[member, q].astype(F32) * row_scale[block]
        high = piece.astype(BF16)
        low = (piece - high.astype(F32)).astype(BF16)
        both = jnp.concatenate([high, low], axis=0)
        wide[...] = lax.dot_general(both, spread[...], (((0,), (0,)), ((), ())), preferred_element_type=F32)

    def work(n, wide, rows_at):
        member, q = where_of(n)
        block = lax.rem(member, NC) * MB + meta_ref[member, 0, q]
        outage = meta_ref[member, 0, SLOTS + q]
        start = pl.multiple_of(block * BLK, BLK)
        own = pl.ds(pl.multiple_of((member // NC) * KC, KC), KC)
        flow_rows[rows_at] = flow_ref[outage, own, :].astype(F32)
        for half in range(KC // 8):
            flows = [flow_rows[rows_at, pl.ds(half * 8 + j, 8, stride=0), :] for j in range(8)]
            sums = [None] * 8
            for i in range(BLK // 8):
                base = scaled[pl.ds(start + i * 8, 8), :]
                total_m = None
                for j in range(8):
                    factor = wide[pl.ds(i * 8, 8), pl.ds((half * 8 + j) * S, S)]
                    post = base + factor * flows[j]
                    square = post * post
                    level = jnp.log2(jnp.exp2(square) + math.e)
                    slope = (level - LOG2E) * jnp.exp2(square - level) * post
                    total_m = slope if total_m is None else total_m + slope
                    part = factor * slope
                    sums[j] = part if sums[j] is None else sums[j] + part
                grad_mon_ref[pl.ds(start + i * 8, 8), :] += total_m
            rows = jnp.concatenate([jnp.sum(v, axis=0, keepdims=True) for v in sums], axis=0)
            place = pl.ds(pl.multiple_of((member // NC) * KC + half * 8, 8), 8)
            grad_out_ref[outage, place, :] += rows

    expand(0, wide_a)

    def pair(p, _):
        expand(2 * p + 1, wide_b)
        work(2 * p, wide_a, 0)

        @pl.when(2 * p + 1 < total)
        def _():
            expand(2 * p + 2, wide_a)
            work(2 * p + 1, wide_b, 1)

        return 0

    lax.fori_loop(0, (total + 1) // 2, pair, 0)
    weight = weights_ref[...] * (4.0 / BLK * math.log(2.0) ** 2)
    grad_mon_ref[...] = grad_mon_ref[...] * column[...] * weight
    grad_out_ref[...] = grad_out_ref[...] * weight[None]


def scatter_kernel(
    mon_ref, flow_ref, grad_mon_ref, grad_out_ref,
    mon_in, relay_in, relay_out, y_in, y_sum, z_in, z_sum, last_in,
    gs, gr, fs, fr, zs, zr, ys, yr,
):
    o, y, z, c = position()
    g, group, along_z, along_y = peers(o, y, z, c)
    signal_all([device for _, device in group + along_z + along_y])
    pl.semaphore_wait(pltpu.get_barrier_semaphore(), len(group) + len(along_z) + len(along_y))

    (up, up_device), (down, down_device) = along_y
    far = lax.rem(y + 2, NY)
    halfway = NZ // 2

    def half(row, part):
        return pl.ds(row * NZ + part * halfway, halfway)

    relays = [
        send(flow_ref.at[half(far, 0)], relay_in.at[0], ys.at[0], yr.at[0], up_device),
        send(flow_ref.at[half(far, 1)], relay_in.at[1], ys.at[1], yr.at[1], down_device),
    ]
    plain = [
        send(flow_ref.at[half(up, 1)], y_in.at[0, 1], ys.at[2], yr.at[2], up_device),
        send(flow_ref.at[half(down, 0)], y_in.at[1, 0], ys.at[3], yr.at[3], down_device),
    ]
    group_hops = []
    for d, (other, device) in enumerate(group):
        rows = pl.ds(pl.multiple_of(lax.rem(other, NC) * MB * BLK + (other // NC) * OWN, 8), OWN)
        group_hops.append(send(mon_ref.at[rows], mon_in.at[d], gs.at[d], gr.at[d], device))
    relays[0].wait()
    relay_out[0] = relay_in[0] + flow_ref[half(up, 0)]
    plain.append(send(relay_out.at[0], y_in.at[0, 0], ys.at[4], yr.at[4], up_device))
    relays[1].wait()
    relay_out[1] = relay_in[1] + flow_ref[half(down, 1)]
    plain.append(send(relay_out.at[1], y_in.at[1, 1], ys.at[5], yr.at[5], down_device))
    for copy in plain:
        copy.wait()
    for part in range(2):
        here = slice(part * halfway, (part + 1) * halfway)
        y_sum[here] = flow_ref[half(y, part)] + y_in[0, part] + y_in[1, part]
    hops = [
        send(y_sum.at[other], z_in.at[d], zs.at[d], zr.at[d], device)
        for d, (other, device) in enumerate(along_z)
    ]
    for copy in group_hops:
        copy.wait()
    rows = pl.ds(pl.multiple_of(c * MB * BLK + o * OWN, 8), OWN)
    total = mon_ref[rows, :]
    for d in range(G - 1):
        total = total + mon_in[d]
    grad_mon_ref[...] = total
    for copy in hops:
        copy.wait()
    total = y_sum[z]
    for d in range(NZ - 1):
        total = total + z_in[d]
    for m in range(G):
        z_sum[m] = total[m * ROWS : (m + 1) * ROWS, :]
    last_in[g] = z_sum[g]
    hops = [
        send(z_sum.at[other], last_in.at[g], fs.at[d], fr.at[d], device)
        for d, (other, device) in enumerate(group)
    ]
    for copy in hops:
        copy.wait()
    for m in range(G):
        grad_out_ref[pl.ds(m * ROWS, ROWS), :] = last_in[m]


def vmem(count):
    return [pl.BlockSpec(memory_space=pltpu.VMEM)] * count


DMA = pltpu.SemaphoreType.DMA


def local(mon_flow, out_flow, rating, weights, lodf, tile_mon, tile_out, tile_count):
    blocks = NY * NZ
    meta = jnp.concatenate(
        [tile_mon[0], tile_out[0], tile_count, jnp.zeros((1, S - 2 * SLOTS - 1), jnp.int32)], axis=1
    )
    tiles, gathered, mon_all, small, meta_all = pl.pallas_call(
        gather_kernel,
        out_shape=(
            jax.ShapeDtypeStruct((G, SLOTS, KC, BLK), BF16),
            jax.ShapeDtypeStruct((blocks, G * ROWS, S), BF16),
            jax.ShapeDtypeStruct((NC, MB * BLK, S), BF16),
            jax.ShapeDtypeStruct((G, 2 * ROWS, S), F32),
            jax.ShapeDtypeStruct((G, 1, S), jnp.int32),
        ),
        in_specs=vmem(5),
        out_specs=tuple(vmem(5)),
        scratch_shapes=[
            pltpu.VMEM((G, SLOTS, KC, BLK), BF16),
            pltpu.VMEM((G, 2 * ROWS, S), F32),
            DMA((3, G - 1)), DMA((3, G - 1)), DMA, DMA,
            DMA((NZ - 1,)), DMA((NZ - 1,)), DMA((2, 3)), DMA((2, 3)),
        ],
        compiler_params=pltpu.CompilerParams(collective_id=0, has_side_effects=True, vmem_limit_bytes=VMEM_BYTES),
        name="gather",
    )(lodf[0, 0], out_flow[0], rating.reshape(MB, BLK), mon_flow, meta)

    part_mon, part_out = pl.pallas_call(
        tile_kernel,
        out_shape=(
            jax.ShapeDtypeStruct((NC * MB * BLK, S), F32),
            jax.ShapeDtypeStruct((blocks, G * ROWS, S), F32),
        ),
        in_specs=[pl.BlockSpec(memory_space=pltpu.SMEM)] + vmem(5),
        out_specs=tuple(vmem(2)),
        scratch_shapes=[
            pltpu.SMEM((G * SLOTS,), jnp.int32),
            pltpu.VMEM((NC * MB * BLK, S), F32),
            pltpu.VMEM((NC * MB * BLK, S), F32),
            pltpu.VMEM((NC * MB, 1, BLK), F32),
            pltpu.VMEM((2 * KC, KC * S), BF16),
            pltpu.VMEM((BLK, KC * S), F32),
            pltpu.VMEM((BLK, KC * S), F32),
            pltpu.VMEM((2, KC, S), F32),
        ],
        compiler_params=pltpu.CompilerParams(vmem_limit_bytes=VMEM_BYTES),
        name="tiles",
    )(meta_all, tiles, gathered, mon_all, small, weights.reshape(1, S))

    grad_mon, grad_out = pl.pallas_call(
        scatter_kernel,
        out_shape=(
            jax.ShapeDtypeStruct((OWN, S), F32),
            jax.ShapeDtypeStruct((G * ROWS, S), F32),
        ),
        in_specs=vmem(2),
        out_specs=tuple(vmem(2)),
        scratch_shapes=[
            pltpu.VMEM((G - 1, OWN, S), F32),
            pltpu.VMEM((2, NZ // 2, G * ROWS, S), F32),
            pltpu.VMEM((2, NZ // 2, G * ROWS, S), F32),
            pltpu.VMEM((2, 2, NZ // 2, G * ROWS, S), F32),
            pltpu.VMEM((NZ, G * ROWS, S), F32),
            pltpu.VMEM((NZ - 1, G * ROWS, S), F32),
            pltpu.VMEM((G, ROWS, S), F32),
            pltpu.VMEM((G, ROWS, S), F32),
            DMA((G - 1,)), DMA((G - 1,)), DMA((G - 1,)), DMA((G - 1,)),
            DMA((NZ - 1,)), DMA((NZ - 1,)), DMA((6,)), DMA((6,)),
        ],
        compiler_params=pltpu.CompilerParams(
            collective_id=1, has_side_effects=True, vmem_limit_bytes=VMEM_BYTES
        ),
        name="scatter",
    )(part_mon, part_out)
    return grad_mon, grad_out[None]


def solution(mesh):
    in_specs = (
        P("mon", None),
        P("out", "mon", None),
        P("mon"),
        P(),
        P("mon", "out", None, None, None),
        P("mon", "out", None),
        P("mon", "out", None),
        P("mon", "out"),
    )
    out_specs = (P(("mon", "out"), None), P("out", "mon", None))
    return jax.shard_map(local, mesh=mesh, in_specs=in_specs, out_specs=out_specs, check_vma=False)
```

```python
import functools
import math

import jax
import jax.numpy as jnp
from jax import lax
from jax.experimental import pallas as pl
from jax.experimental.pallas import tpu as pltpu
from jax.sharding import PartitionSpec as P

MESH = pl.DeviceIdType.MESH
NX, NY, NZ, NC = 4, 4, 8, 2
NP = NY // 2
SAME = 2 * NX
G = SAME * NC
BLK = 128
S = 128
SLOTS = 8
KC = BLK // G
MB = 3
UNITS = 2 * NC * MB
SETS = NP * NZ * SAME
OWN = MB * BLK // NX
LOG2E = math.log2(math.e)
VMEM_BYTES = 56 << 20
F32 = jnp.float32
BF16 = jnp.bfloat16


def position():
    i = lax.axis_index("mon")
    o = lax.axis_index("out")
    c = lax.rem(i, NC)
    z = lax.rem(i // NC, NZ)
    y = i // (NC * NZ)
    p = y // 2
    return o, p, lax.rem(y + p, 2), z, c


def at(o, p, e, z, c):
    y = 2 * p + lax.rem(e + p, 2)
    return ((y * NZ + z) * NC + c, o)


def peers(o, p, e, z, c):
    own = (c * 2 + e) * NX + o
    group = []
    for d in range(1, G):
        other = lax.rem(own + d, G)
        oo, oe, oc = lax.rem(other, NX), lax.rem(other // NX, 2), other // SAME
        group.append((other, oo, oe, oc, at(oo, p, oe, z, oc)))
    same = []
    for d in range(1, SAME):
        other = lax.rem(e * NX + o + d, SAME)
        same.append((other, at(lax.rem(other, NX), p, other // NX, z, c)))
    along_z = {}
    for d in range(1, NZ):
        other = lax.rem(z + d, NZ)
        along_z[d] = (other, at(o, p, e, other, c))
    return own, group, same, along_z, at(o, 1 - p, e, z, c)


def enter(group, along_z, across):
    barrier = pltpu.get_barrier_semaphore()
    devices = [entry[-1] for entry in group] + [device for _, device in along_z.values()] + [across]
    for device in devices:
        pl.semaphore_signal(barrier, inc=1, device_id=device, device_id_type=MESH)
    return len(devices)


def send(src, dst, send_sem, recv_sem, device):
    copy = pltpu.make_async_remote_copy(
        src_ref=src, dst_ref=dst, send_sem=send_sem, recv_sem=recv_sem, device_id=device, device_id_type=MESH
    )
    copy.start()
    return copy


def gather_kernel(
    lodf_ref, flow_ref, rating_ref, mon_ref, meta_ref,
    tiles_ref, gathered_ref, mon_all_ref, rating_all_ref, meta_all_ref,
    tiles_out, flow_out, flow_in, gs, gr, fs, fr, ms, mr, zs, zr, ys, yr,
):
    o, p, e, z, c = position()
    own, group, same, along_z, across = peers(o, p, e, z, c)
    signals = enter(group, along_z, across)
    place = e * NX + o
    unit = e * NC + c
    flow_out[...] = flow_ref[...].astype(F32).reshape(SAME, KC, S)
    flow_in[place] = flow_out[place]
    for q in range(0, SLOTS, 2):
        first = jnp.transpose(lodf_ref[q].astype(F32))
        second = jnp.transpose(lodf_ref[q + 1].astype(F32))
        for m in range(G):
            rows = slice(m * KC, (m + 1) * KC)
            tiles_out[m, q * KC : (q + 2) * KC, :] = jnp.concatenate([first[rows], second[rows]], axis=0).astype(BF16)
    tiles_ref[own] = tiles_out[own]
    meta_all_ref[own] = meta_ref[...]
    mon_all_ref[unit] = mon_ref[...]
    rating_all_ref[unit] = rating_ref[...]

    pl.semaphore_wait(pltpu.get_barrier_semaphore(), signals)
    flows = [
        send(flow_out.at[other], flow_in.at[place], fs.at[d], fr.at[d], device)
        for d, (other, device) in enumerate(same)
    ]
    rest = []
    for d, (other, _, _, _, device) in enumerate(group):
        rest.append(send(tiles_out.at[other], tiles_ref.at[own], gs.at[0, d], gr.at[0, d], device))
    for d, (other, _, _, _, device) in enumerate(group):
        rest.append(send(meta_ref, meta_all_ref.at[own], gs.at[1, d], gr.at[1, d], device))
    for d in range(1, 2 * NC):
        other = lax.rem(unit + d, 2 * NC)
        device = at(o, p, other // NC, z, lax.rem(other, NC))
        rest.append(send(mon_ref, mon_all_ref.at[unit], ms.at[0, d - 1], mr.at[0, d - 1], device))
        rest.append(send(rating_ref, rating_all_ref.at[unit], ms.at[1, d - 1], mr.at[1, d - 1], device))
    for copy in flows:
        copy.wait()
    mine = p * NZ + z
    gathered_ref[mine] = flow_in[...].reshape(SAME * KC, S).astype(BF16)
    block = gathered_ref.at[mine]
    hops = {}
    for d in (4, 3, 5, 2, 6, 1, 7):
        hops[d] = send(block, block, zs.at[d - 1], zr.at[d - 1], along_z[d][1])
    crossed = [send(block, block, ys.at[0], yr.at[0], across)]
    for d in (1, 7, 2, 6, 3, 5, 4):
        hops[d].wait_recv()
        block = gathered_ref.at[p * NZ + lax.rem(z + NZ - d, NZ)]
        crossed.append(send(block, block, ys.at[d], yr.at[d], across))
    for copy in hops.values():
        copy.wait_send()
    for copy in rest + crossed:
        copy.wait()


def tile_kernel(
    meta_ref, tiles_ref, flow_ref, mon_ref, rating_ref, weights_ref,
    grad_mon_ref, grad_out_ref,
    from_list, block_list, set_list, scaled, column, row_scale, spread, pieces, flows, wide_a, wide_b,
):
    for u in range(2 * NC):
        for t in range(MB):
            b = u * MB + t
            scale = math.sqrt(LOG2E) / rating_ref[u, t : t + 1, :]
            row_scale[b, :, :] = scale
            turned = jnp.transpose(jnp.broadcast_to(scale, (BLK, BLK)))
            column[b * BLK : (b + 1) * BLK, :] = turned
            scaled[b * BLK : (b + 1) * BLK, :] = turned * mon_ref[u, t * BLK : (t + 1) * BLK, :].astype(F32)
    row_scale[UNITS, :, :] = jnp.zeros((1, BLK), F32)
    scaled[UNITS * BLK :, :] = jnp.zeros((BLK, S), F32)
    grad_mon_ref[...] = jnp.zeros_like(grad_mon_ref)
    grad_out_ref[...] = jnp.zeros_like(grad_out_ref)
    pieces[...] = tiles_ref[...].astype(F32).reshape(G * SLOTS, KC, BLK)
    flows[0:SETS] = flow_ref[...].astype(F32).reshape(SETS, KC, S)
    flows[SETS] = jnp.zeros((KC, S), F32)
    term = lax.broadcasted_iota(jnp.int32, spread.shape, 0)
    lane = lax.broadcasted_iota(jnp.int32, spread.shape, 1)
    spread[...] = jnp.where(lax.rem(term, KC) == lane // S, 1.0, 0.0).astype(BF16)

    def list_member(member, total):
        count = meta_ref[member, 0, 2 * SLOTS]
        unit = lax.rem(member // NX, 2) * NC + member // SAME
        out = lax.rem(member, NX)

        def add(q, _):
            block = meta_ref[member, 0, SLOTS + q]
            y = block // NZ
            p = y // 2
            row = (p * NZ + lax.rem(block, NZ)) * SAME + lax.rem(y + p, 2) * NX + out
            from_list[total + q] = member * SLOTS + q
            block_list[total + q] = unit * MB + meta_ref[member, 0, q]
            set_list[total + q] = row
            return 0

        lax.fori_loop(0, count, add, 0)
        return total + count

    total = lax.fori_loop(0, G, list_member, 0)
    for extra in range(3):
        from_list[total + extra] = 0
        block_list[total + extra] = UNITS
        set_list[total + extra] = SETS

    def expand(n, wide):
        piece = pieces[from_list[n]] * row_scale[block_list[n]]
        high = piece.astype(BF16).astype(F32)
        both = jnp.concatenate([high, piece - high], axis=0).astype(BF16)
        wide[...] = lax.dot_general(both, spread[...], (((0,), (0,)), ((), ())), preferred_element_type=F32)

    def work(n, wide):
        row = set_list[n]
        start = pl.multiple_of(block_list[n] * BLK, BLK)
        flow = [flows[row, pl.ds(j, 8, stride=0), :] for j in range(KC)]
        sums = [None] * KC
        for i in range(BLK // 8):
            base = scaled[pl.ds(start + i * 8, 8), :]
            total_m = None
            for j in range(KC):
                factor = wide[i * 8 : (i + 1) * 8, j * S : (j + 1) * S]
                post = base + factor * flow[j]
                square = post * post
                level = jnp.log2(jnp.exp2(square) + math.e)
                slope = (level - LOG2E) * jnp.exp2(square - level) * post
                total_m = slope if total_m is None else total_m + slope
                part = factor * slope
                sums[j] = part if sums[j] is None else sums[j] + part
            grad_mon_ref[pl.ds(start + i * 8, 8), :] += total_m
        grad_out_ref[row] += jnp.concatenate([jnp.sum(v, axis=0, keepdims=True) for v in sums], axis=0)

    expand(0, wide_a)

    def pair(n, _):
        expand(2 * n + 1, wide_b)
        work(2 * n, wide_a)
        expand(2 * n + 2, wide_a)
        work(2 * n + 1, wide_b)
        return 0

    lax.fori_loop(0, (total + 1) // 2, pair, 0)
    weight = weights_ref[...] * (4.0 / BLK * math.log(2.0) ** 2)
    grad_mon_ref[0 : UNITS * BLK, :] = grad_mon_ref[0 : UNITS * BLK, :] * column[...] * weight
    grad_out_ref[...] = grad_out_ref[...] * weight[None]


def scatter_kernel(
    mon_ref, flow_ref, grad_mon_ref, grad_out_ref,
    mon_in, y_in, y_sum, z_in, z_sum, last_in,
    gs, gr, fs, fr, zs, zr, ys, yr,
):
    o, p, e, z, c = position()
    own, group, same, along_z, across = peers(o, p, e, z, c)
    place = e * NX + o
    signals = enter(group, along_z, across)
    pl.semaphore_wait(pltpu.get_barrier_semaphore(), signals)

    order = (4, 3, 5, 2, 6, 1, 7, 0)
    crossed = {}
    for d in order:
        there = pl.ds(((1 - p) * NZ + lax.rem(z + d, NZ)) * SAME, SAME)
        crossed[d] = send(flow_ref.at[there], y_in.at[d], ys.at[d], yr.at[d], across)
    group_hops = []
    for d, (other, oo, oe, oc, device) in enumerate(group):
        rows = pl.ds(pl.multiple_of((oe * NC + oc) * MB * BLK + oo * OWN, 8), OWN)
        group_hops.append(send(mon_ref.at[rows], mon_in.at[d], gs.at[d], gr.at[d], device))
    hops = []
    for d in order:
        crossed[d].wait()
        here = pl.ds((p * NZ + lax.rem(z + d, NZ)) * SAME, SAME)
        y_sum[d] = flow_ref[here] + y_in[d]
        if d > 0:
            hops.append(send(y_sum.at[d], z_in.at[d - 1], zs.at[d - 1], zr.at[d - 1], along_z[d][1]))
    for copy in hops:
        copy.wait()
    total = y_sum[0]
    for d in range(NZ - 1):
        total = total + z_in[d]
    z_sum[...] = total
    last_in[place] = z_sum[place]
    hops = [
        send(z_sum.at[other], last_in.at[place], fs.at[d], fr.at[d], device)
        for d, (other, device) in enumerate(same)
    ]
    for copy in group_hops:
        copy.wait()
    rows = pl.ds(pl.multiple_of((e * NC + c) * MB * BLK + o * OWN, 8), OWN)
    total = mon_ref[rows, :]
    for d in range(G - 1):
        total = total + mon_in[d]
    grad_mon_ref[...] = total
    for copy in hops:
        copy.wait()
    for m in range(SAME):
        grad_out_ref[m * KC : (m + 1) * KC, :] = last_in[m]


def vmem(count):
    return [pl.BlockSpec(memory_space=pltpu.VMEM)] * count


DMA = pltpu.SemaphoreType.DMA


def local(mon_flow, out_flow, rating, weights, lodf, tile_mon, tile_out, tile_count):
    meta = jnp.concatenate(
        [tile_mon[0], tile_out[0], tile_count, jnp.zeros((1, S - 2 * SLOTS - 1), jnp.int32)], axis=1
    )
    tiles, gathered, mon_all, ratings, meta_all = pl.pallas_call(
        gather_kernel,
        out_shape=(
            jax.ShapeDtypeStruct((G, SLOTS * KC, BLK), BF16),
            jax.ShapeDtypeStruct((NP * NZ, SAME * KC, S), BF16),
            jax.ShapeDtypeStruct((2 * NC, MB * BLK, S), BF16),
            jax.ShapeDtypeStruct((2 * NC, MB, BLK), F32),
            jax.ShapeDtypeStruct((G, 1, S), jnp.int32),
        ),
        in_specs=vmem(5),
        out_specs=tuple(vmem(5)),
        scratch_shapes=[
            pltpu.VMEM((G, SLOTS * KC, BLK), BF16),
            pltpu.VMEM((SAME, KC, S), F32),
            pltpu.VMEM((SAME, KC, S), F32),
            DMA((2, G - 1)), DMA((2, G - 1)), DMA((SAME - 1,)), DMA((SAME - 1,)),
            DMA((2, 2 * NC - 1)), DMA((2, 2 * NC - 1)), DMA((NZ - 1,)), DMA((NZ - 1,)), DMA((NZ,)), DMA((NZ,)),
        ],
        compiler_params=pltpu.CompilerParams(collective_id=0, has_side_effects=True, vmem_limit_bytes=VMEM_BYTES),
        name="gather",
    )(lodf[0, 0], out_flow[0], rating.reshape(MB, BLK), mon_flow, meta)

    part_mon, part_out = pl.pallas_call(
        tile_kernel,
        out_shape=(
            jax.ShapeDtypeStruct(((UNITS + 1) * BLK, S), F32),
            jax.ShapeDtypeStruct((SETS + 1, KC, S), F32),
        ),
        in_specs=[pl.BlockSpec(memory_space=pltpu.SMEM)] + vmem(5),
        out_specs=tuple(vmem(2)),
        scratch_shapes=[
            pltpu.SMEM((G * SLOTS + 8,), jnp.int32),
            pltpu.SMEM((G * SLOTS + 8,), jnp.int32),
            pltpu.SMEM((G * SLOTS + 8,), jnp.int32),
            pltpu.VMEM(((UNITS + 1) * BLK, S), F32),
            pltpu.VMEM((UNITS * BLK, S), F32),
            pltpu.VMEM((UNITS + 1, 1, BLK), F32),
            pltpu.VMEM((2 * KC, KC * S), BF16),
            pltpu.VMEM((G * SLOTS, KC, BLK), F32),
            pltpu.VMEM((SETS + 1, KC, S), F32),
            pltpu.VMEM((BLK, KC * S), F32),
            pltpu.VMEM((BLK, KC * S), F32),
        ],
        compiler_params=pltpu.CompilerParams(vmem_limit_bytes=VMEM_BYTES),
        name="tiles",
    )(meta_all, tiles, gathered, mon_all, ratings, weights.reshape(1, S))

    grad_mon, grad_out = pl.pallas_call(
        scatter_kernel,
        out_shape=(
            jax.ShapeDtypeStruct((OWN, S), F32),
            jax.ShapeDtypeStruct((SAME * KC, S), F32),
        ),
        in_specs=vmem(2),
        out_specs=tuple(vmem(2)),
        scratch_shapes=[
            pltpu.VMEM((G - 1, OWN, S), F32),
            pltpu.VMEM((NZ, SAME, KC, S), F32),
            pltpu.VMEM((NZ, SAME, KC, S), F32),
            pltpu.VMEM((NZ - 1, SAME, KC, S), F32),
            pltpu.VMEM((SAME, KC, S), F32),
            pltpu.VMEM((SAME, KC, S), F32),
            DMA((G - 1,)), DMA((G - 1,)), DMA((SAME - 1,)), DMA((SAME - 1,)),
            DMA((NZ - 1,)), DMA((NZ - 1,)), DMA((NZ,)), DMA((NZ,)),
        ],
        compiler_params=pltpu.CompilerParams(
            collective_id=1, has_side_effects=True, vmem_limit_bytes=VMEM_BYTES
        ),
        name="scatter",
    )(part_mon, part_out)
    return grad_mon, grad_out[None]


def solution(mesh):
    in_specs = (
        P("mon", None),
        P("out", "mon", None),
        P("mon"),
        P(),
        P("mon", "out", None, None, None),
        P("mon", "out", None),
        P("mon", "out", None),
        P("mon", "out"),
    )
    out_specs = (P(("mon", "out"), None), P("out", "mon", None))
    return jax.shard_map(local, mesh=mesh, in_specs=in_specs, out_specs=out_specs, check_vma=False)
```

```python
import functools
import math

import jax
import jax.numpy as jnp
from jax import lax
from jax.experimental import pallas as pl
from jax.experimental.pallas import tpu as pltpu
from jax.sharding import PartitionSpec as P

MESH = pl.DeviceIdType.MESH
NX, NY, NZ, NC = 4, 4, 8, 2
NP = NY // 2
SAME = 2 * NX
G = SAME * NC
BLK = 128
S = 128
SLOTS = 8
KC = BLK // G
MB = 3
UNITS = 2 * NC * MB
SETS = NP * NZ * SAME
OWN = MB * BLK // NX
LOG2E = math.log2(math.e)
VMEM_BYTES = 16 << 20
F32 = jnp.float32
BF16 = jnp.bfloat16


def position():
    i = lax.axis_index("mon")
    o = lax.axis_index("out")
    c = lax.rem(i, NC)
    z = lax.rem(i // NC, NZ)
    y = i // (NC * NZ)
    p = y // 2
    return o, p, lax.rem(y + p, 2), z, c


def at(o, p, e, z, c):
    y = 2 * p + lax.rem(e + p, 2)
    return ((y * NZ + z) * NC + c, o)


def peers(o, p, e, z, c):
    own = (c * 2 + e) * NX + o
    group = []
    for d in range(1, G):
        other = lax.rem(own + d, G)
        oo, oe, oc = lax.rem(other, NX), lax.rem(other // NX, 2), other // SAME
        group.append((other, oo, oe, oc, at(oo, p, oe, z, oc)))
    same = []
    for d in range(1, SAME):
        other = lax.rem(e * NX + o + d, SAME)
        same.append((other, at(lax.rem(other, NX), p, other // NX, z, c)))
    along_z = {}
    for d in range(1, NZ):
        other = lax.rem(z + d, NZ)
        along_z[d] = (other, at(o, p, e, other, c))
    return own, group, same, along_z, at(o, 1 - p, e, z, c)


def enter(group, along_z, across):
    barrier = pltpu.get_barrier_semaphore()
    devices = [entry[-1] for entry in group] + [device for _, device in along_z.values()] + [across]
    for device in devices:
        pl.semaphore_signal(barrier, inc=1, device_id=device, device_id_type=MESH)
    return len(devices)


def send(src, dst, send_sem, recv_sem, device):
    copy = pltpu.make_async_remote_copy(
        src_ref=src, dst_ref=dst, send_sem=send_sem, recv_sem=recv_sem, device_id=device, device_id_type=MESH
    )
    copy.start()
    return copy


def gather_kernel(
    count_ref, tile_mon_hbm, tile_out_hbm, lodf_hbm, flow_hbm, rating_hbm, mon_hbm,
    tiles_ref, gathered_ref, mon_all_ref, rating_all_ref, meta_all_ref,
    tile_mon_ref, tile_out_ref, lodf_ref, flow_ref, tiles_out, flow_out, flow_in, loads, gs, gr, fs, fr, ms, mr, zs, zr, ys, yr,
):
    o, p, e, z, c = position()
    place = e * NX + o
    unit = e * NC + c
    load_flow = pltpu.make_async_copy(flow_hbm, flow_ref, loads.at[0])
    load_lodf = pltpu.make_async_copy(lodf_hbm, lodf_ref, loads.at[1])
    load_mon = pltpu.make_async_copy(mon_hbm, mon_all_ref.at[unit], loads.at[2])
    load_rating = pltpu.make_async_copy(rating_hbm, rating_all_ref.at[unit], loads.at[3])
    words_in = [
        pltpu.make_async_copy(tile_mon_hbm, tile_mon_ref, loads.at[4]),
        pltpu.make_async_copy(tile_out_hbm, tile_out_ref, loads.at[5]),
    ]
    for load in [load_flow, load_lodf, load_mon, load_rating] + words_in:
        load.start()
    own, group, same, along_z, across = peers(o, p, e, z, c)
    signals = enter(group, along_z, across)
    for load in words_in:
        load.wait()
    lane = lax.broadcasted_iota(jnp.int32, (1, S), 1)
    words = jnp.where(lane == 2 * SLOTS, count_ref[0, 0], 0)
    for q in range(SLOTS):
        block = tile_out_ref[0, q]
        across_y = block // NZ
        pair = across_y // 2
        row = (pair * NZ + lax.rem(block, NZ)) * SAME + lax.rem(across_y + pair, 2) * NX + o
        words = jnp.where(lane == q, unit * MB + tile_mon_ref[0, q], words)
        words = jnp.where(lane == SLOTS + q, row, words)
    meta_all_ref[own] = words
    load_flow.wait()
    flow_out[...] = flow_ref[...].astype(F32).reshape(SAME, KC, S)
    flow_in[place] = flow_out[place]
    load_lodf.wait()
    for q in range(0, SLOTS, 2):
        first = jnp.transpose(lodf_ref[q].astype(F32))
        second = jnp.transpose(lodf_ref[q + 1].astype(F32))
        for m in range(G):
            rows = slice(m * KC, (m + 1) * KC)
            tiles_out[m, q * KC : (q + 2) * KC, :] = jnp.concatenate([first[rows], second[rows]], axis=0).astype(BF16)
    tiles_ref[own] = tiles_out[own]
    load_mon.wait()
    load_rating.wait()

    pl.semaphore_wait(pltpu.get_barrier_semaphore(), signals)
    flows = [
        send(flow_out.at[other], flow_in.at[place], fs.at[d], fr.at[d], device)
        for d, (other, device) in enumerate(same)
    ]
    rest = []
    for d, (other, _, _, _, device) in enumerate(group):
        rest.append(send(tiles_out.at[other], tiles_ref.at[own], gs.at[0, d], gr.at[0, d], device))
    for d, (other, _, _, _, device) in enumerate(group):
        rest.append(send(meta_all_ref.at[own], meta_all_ref.at[own], gs.at[1, d], gr.at[1, d], device))
    for d in range(1, 2 * NC):
        other = lax.rem(unit + d, 2 * NC)
        device = at(o, p, other // NC, z, lax.rem(other, NC))
        rest.append(send(mon_all_ref.at[unit], mon_all_ref.at[unit], ms.at[0, d - 1], mr.at[0, d - 1], device))
        rest.append(send(rating_all_ref.at[unit], rating_all_ref.at[unit], ms.at[1, d - 1], mr.at[1, d - 1], device))
    for copy in flows:
        copy.wait()
    mine = p * NZ + z
    gathered_ref[mine] = flow_in[...].reshape(SAME * KC, S).astype(BF16)
    block = gathered_ref.at[mine]
    hops = {}
    for d in (4, 3, 5, 2, 6, 1, 7):
        hops[d] = send(block, block, zs.at[d - 1], zr.at[d - 1], along_z[d][1])
    crossed = [send(block, block, ys.at[0], yr.at[0], across)]
    for d in (1, 7, 2, 6, 3, 5, 4):
        hops[d].wait_recv()
        block = gathered_ref.at[p * NZ + lax.rem(z + NZ - d, NZ)]
        crossed.append(send(block, block, ys.at[d], yr.at[d], across))
    for copy in hops.values():
        copy.wait_send()
    for copy in rest + crossed:
        copy.wait()


def tile_kernel(
    meta_ref, tiles_ref, flow_ref, mon_ref, rating_ref, weights_hbm,
    grad_mon_ref, grad_out_ref,
    from_list, block_list, set_list, weights_ref, load, scaled, column, row_scale, spread, pieces, flows, wide_a, wide_b,
):
    load_weights = pltpu.make_async_copy(weights_hbm, weights_ref, load)
    load_weights.start()
    for u in range(2 * NC):
        for t in range(MB):
            b = u * MB + t
            scale = math.sqrt(LOG2E) / rating_ref[u, t : t + 1, :]
            row_scale[b, :, :] = scale
            turned = jnp.transpose(jnp.broadcast_to(scale, (BLK, BLK)))
            column[b * BLK : (b + 1) * BLK, :] = turned
            scaled[b * BLK : (b + 1) * BLK, :] = turned * mon_ref[u, t * BLK : (t + 1) * BLK, :].astype(F32)
    row_scale[UNITS, :, :] = jnp.zeros((1, BLK), F32)
    scaled[UNITS * BLK :, :] = jnp.zeros((BLK, S), F32)
    grad_mon_ref[...] = jnp.zeros_like(grad_mon_ref)
    grad_out_ref[...] = jnp.zeros_like(grad_out_ref)
    pieces[...] = tiles_ref[...].astype(F32).reshape(G * SLOTS, KC, BLK)
    flows[0:SETS] = flow_ref[...].astype(F32).reshape(SETS, KC, S)
    flows[SETS] = jnp.zeros((KC, S), F32)
    term = lax.broadcasted_iota(jnp.int32, spread.shape, 0)
    lane = lax.broadcasted_iota(jnp.int32, spread.shape, 1)
    spread[...] = jnp.where(lax.rem(term, KC) == lane // S, 1.0, 0.0).astype(BF16)

    def list_member(member, total):
        count = meta_ref[member, 0, 2 * SLOTS]

        def add(q, _):
            from_list[total + q] = member * SLOTS + q
            block_list[total + q] = meta_ref[member, 0, q]
            set_list[total + q] = meta_ref[member, 0, SLOTS + q]
            return 0

        lax.fori_loop(0, count, add, 0)
        return total + count

    total = lax.fori_loop(0, G, list_member, 0)
    for extra in range(3):
        from_list[total + extra] = 0
        block_list[total + extra] = UNITS
        set_list[total + extra] = SETS

    def expand(n, wide):
        piece = pieces[from_list[n]] * row_scale[block_list[n]]
        high = piece.astype(BF16).astype(F32)
        both = jnp.concatenate([high, piece - high], axis=0).astype(BF16)
        wide[...] = lax.dot_general(both, spread[...], (((0,), (0,)), ((), ())), preferred_element_type=F32)

    def work(n, wide):
        row = set_list[n]
        start = pl.multiple_of(block_list[n] * BLK, BLK)
        flow = [flows[row, pl.ds(j, 8, stride=0), :] for j in range(KC)]
        sums = [None] * KC
        for i in range(BLK // 8):
            base = scaled[pl.ds(start + i * 8, 8), :]
            total_m = None
            for j in range(KC):
                factor = wide[i * 8 : (i + 1) * 8, j * S : (j + 1) * S]
                post = base + factor * flow[j]
                square = post * post
                level = jnp.log2(jnp.exp2(square) + math.e)
                slope = (level - LOG2E) * jnp.exp2(square - level) * post
                total_m = slope if total_m is None else total_m + slope
                part = factor * slope
                sums[j] = part if sums[j] is None else sums[j] + part
            grad_mon_ref[pl.ds(start + i * 8, 8), :] += total_m
        grad_out_ref[row] += jnp.concatenate([jnp.sum(v, axis=0, keepdims=True) for v in sums], axis=0)

    expand(0, wide_a)

    def pair(n, _):
        expand(2 * n + 1, wide_b)
        work(2 * n, wide_a)
        expand(2 * n + 2, wide_a)
        work(2 * n + 1, wide_b)
        return 0

    lax.fori_loop(0, (total + 1) // 2, pair, 0)
    load_weights.wait()
    weight = weights_ref[...] * (4.0 / BLK * math.log(2.0) ** 2)
    grad_mon_ref[0 : UNITS * BLK, :] = grad_mon_ref[0 : UNITS * BLK, :] * column[...] * weight
    grad_out_ref[...] = grad_out_ref[...] * weight[None]


def scatter_kernel(
    mon_ref, flow_ref, grad_mon_ref, grad_out_ref,
    mon_in, y_in, y_sum, z_in, z_sum, last_in,
    gs, gr, fs, fr, zs, zr, ys, yr,
):
    o, p, e, z, c = position()
    own, group, same, along_z, across = peers(o, p, e, z, c)
    place = e * NX + o
    signals = enter(group, along_z, across)
    pl.semaphore_wait(pltpu.get_barrier_semaphore(), signals)

    order = (4, 3, 5, 2, 6, 1, 7, 0)
    crossed = {}
    for d in order:
        there = pl.ds(((1 - p) * NZ + lax.rem(z + d, NZ)) * SAME, SAME)
        crossed[d] = send(flow_ref.at[there], y_in.at[d], ys.at[d], yr.at[d], across)
    group_hops = []
    for d, (other, oo, oe, oc, device) in enumerate(group):
        rows = pl.ds(pl.multiple_of((oe * NC + oc) * MB * BLK + oo * OWN, 8), OWN)
        group_hops.append(send(mon_ref.at[rows], mon_in.at[d], gs.at[d], gr.at[d], device))
    hops = []
    for d in order:
        crossed[d].wait()
        here = pl.ds((p * NZ + lax.rem(z + d, NZ)) * SAME, SAME)
        y_sum[d] = flow_ref[here] + y_in[d]
        if d > 0:
            hops.append(send(y_sum.at[d], z_in.at[d - 1], zs.at[d - 1], zr.at[d - 1], along_z[d][1]))
    for copy in hops:
        copy.wait()
    total = y_sum[0]
    for d in range(NZ - 1):
        total = total + z_in[d]
    z_sum[...] = total
    last_in[place] = z_sum[place]
    hops = [
        send(z_sum.at[other], last_in.at[place], fs.at[d], fr.at[d], device)
        for d, (other, device) in enumerate(same)
    ]
    for copy in group_hops:
        copy.wait()
    rows = pl.ds(pl.multiple_of((e * NC + c) * MB * BLK + o * OWN, 8), OWN)
    total = mon_ref[rows, :]
    for d in range(G - 1):
        total = total + mon_in[d]
    grad_mon_ref[...] = total
    for copy in hops:
        copy.wait()
    for m in range(SAME):
        grad_out_ref[m * KC : (m + 1) * KC, :] = last_in[m]


def vmem(count):
    return [pl.BlockSpec(memory_space=pltpu.VMEM)] * count


DMA = pltpu.SemaphoreType.DMA


def local(mon_flow, out_flow, rating, weights, lodf, tile_mon, tile_out, tile_count):
    inputs = [
        tile_mon[0], tile_out[0],
        lodf[0, 0], out_flow[0], rating.reshape(MB, BLK), mon_flow, weights.reshape(1, S),
    ]
    inputs = [pltpu.with_memory_space_constraint(x, pltpu.HBM) for x in inputs]
    tiles, gathered, mon_all, ratings, meta_all = pl.pallas_call(
        gather_kernel,
        out_shape=(
            jax.ShapeDtypeStruct((G, SLOTS * KC, BLK), BF16),
            jax.ShapeDtypeStruct((NP * NZ, SAME * KC, S), BF16),
            jax.ShapeDtypeStruct((2 * NC, MB * BLK, S), BF16),
            jax.ShapeDtypeStruct((2 * NC, MB, BLK), F32),
            jax.ShapeDtypeStruct((G, 1, S), jnp.int32),
        ),
        in_specs=[pl.BlockSpec(memory_space=pltpu.SMEM)] + [pl.BlockSpec(memory_space=pltpu.HBM)] * 6,
        out_specs=tuple(vmem(5)),
        scratch_shapes=[
            pltpu.SMEM((1, SLOTS), jnp.int32),
            pltpu.SMEM((1, SLOTS), jnp.int32),
            pltpu.VMEM((SLOTS, BLK, BLK), BF16),
            pltpu.VMEM((SAME * KC, S), BF16),
            pltpu.VMEM((G, SLOTS * KC, BLK), BF16),
            pltpu.VMEM((SAME, KC, S), F32),
            pltpu.VMEM((SAME, KC, S), F32),
            DMA((6,)), DMA((2, G - 1)), DMA((2, G - 1)), DMA((SAME - 1,)), DMA((SAME - 1,)),
            DMA((2, 2 * NC - 1)), DMA((2, 2 * NC - 1)), DMA((NZ - 1,)), DMA((NZ - 1,)), DMA((NZ,)), DMA((NZ,)),
        ],
        compiler_params=pltpu.CompilerParams(collective_id=0, has_side_effects=True, vmem_limit_bytes=VMEM_BYTES),
        name="gather",
    )(tile_count, *inputs[:6])

    part_mon, part_out = pl.pallas_call(
        tile_kernel,
        out_shape=(
            jax.ShapeDtypeStruct(((UNITS + 1) * BLK, S), F32),
            jax.ShapeDtypeStruct((SETS + 1, KC, S), F32),
        ),
        in_specs=[pl.BlockSpec(memory_space=pltpu.SMEM)] + vmem(4) + [pl.BlockSpec(memory_space=pltpu.HBM)],
        out_specs=tuple(vmem(2)),
        scratch_shapes=[
            pltpu.SMEM((G * SLOTS + 8,), jnp.int32),
            pltpu.SMEM((G * SLOTS + 8,), jnp.int32),
            pltpu.SMEM((G * SLOTS + 8,), jnp.int32),
            pltpu.VMEM((1, S), F32),
            DMA,
            pltpu.VMEM(((UNITS + 1) * BLK, S), F32),
            pltpu.VMEM((UNITS * BLK, S), F32),
            pltpu.VMEM((UNITS + 1, 1, BLK), F32),
            pltpu.VMEM((2 * KC, KC * S), BF16),
            pltpu.VMEM((G * SLOTS, KC, BLK), F32),
            pltpu.VMEM((SETS + 1, KC, S), F32),
            pltpu.VMEM((BLK, KC * S), F32),
            pltpu.VMEM((BLK, KC * S), F32),
        ],
        compiler_params=pltpu.CompilerParams(vmem_limit_bytes=VMEM_BYTES),
        name="tiles",
    )(meta_all, tiles, gathered, mon_all, ratings, inputs[6])

    grad_mon, grad_out = pl.pallas_call(
        scatter_kernel,
        out_shape=(
            jax.ShapeDtypeStruct((OWN, S), F32),
            jax.ShapeDtypeStruct((SAME * KC, S), F32),
        ),
        in_specs=vmem(2),
        out_specs=tuple(vmem(2)),
        scratch_shapes=[
            pltpu.VMEM((G - 1, OWN, S), F32),
            pltpu.VMEM((NZ, SAME, KC, S), F32),
            pltpu.VMEM((NZ, SAME, KC, S), F32),
            pltpu.VMEM((NZ - 1, SAME, KC, S), F32),
            pltpu.VMEM((SAME, KC, S), F32),
            pltpu.VMEM((SAME, KC, S), F32),
            DMA((G - 1,)), DMA((G - 1,)), DMA((SAME - 1,)), DMA((SAME - 1,)),
            DMA((NZ - 1,)), DMA((NZ - 1,)), DMA((NZ,)), DMA((NZ,)),
        ],
        compiler_params=pltpu.CompilerParams(
            collective_id=1, has_side_effects=True, vmem_limit_bytes=VMEM_BYTES
        ),
        name="scatter",
    )(part_mon, part_out)
    return grad_mon, grad_out[None]


def solution(mesh):
    in_specs = (
        P("mon", None),
        P("out", "mon", None),
        P("mon"),
        P(),
        P("mon", "out", None, None, None),
        P("mon", "out", None),
        P("mon", "out", None),
        P("mon", "out"),
    )
    out_specs = (P(("mon", "out"), None), P("out", "mon", None))
    return jax.shard_map(local, mesh=mesh, in_specs=in_specs, out_specs=out_specs, check_vma=False)
```

```python
import functools
import math

import jax
import jax.numpy as jnp
from jax import lax
from jax.experimental import pallas as pl
from jax.experimental.pallas import tpu as pltpu
from jax.sharding import PartitionSpec as P

MESH = pl.DeviceIdType.MESH
NX, NY, NZ, NC = 4, 4, 8, 2
NP = NY // 2
SAME = 2 * NX
G = SAME * NC
BLK = 128
S = 128
SLOTS = 8
KC = BLK // G
MB = 3
UNROLL = 8
UNITS = 2 * NC * MB
SETS = NP * NZ * SAME
OWN = MB * BLK // NX
LOG2E = math.log2(math.e)
VMEM_BYTES = 16 << 20
F32 = jnp.float32
BF16 = jnp.bfloat16


def position():
    i = lax.axis_index("mon")
    o = lax.axis_index("out")
    c = lax.rem(i, NC)
    z = lax.rem(i // NC, NZ)
    y = i // (NC * NZ)
    p = y // 2
    return o, p, lax.rem(y + p, 2), z, c


def at(o, p, e, z, c):
    y = 2 * p + lax.rem(e + p, 2)
    return ((y * NZ + z) * NC + c, o)


def peers(o, p, e, z, c):
    own = (c * 2 + e) * NX + o
    group = []
    for d in range(1, G):
        other = lax.rem(own + d, G)
        oo, oe, oc = lax.rem(other, NX), lax.rem(other // NX, 2), other // SAME
        group.append((other, oo, oe, oc, at(oo, p, oe, z, oc)))
    same = []
    for d in range(1, SAME):
        other = lax.rem(e * NX + o + d, SAME)
        same.append((other, at(lax.rem(other, NX), p, other // NX, z, c)))
    along_z = {}
    for d in range(1, NZ):
        other = lax.rem(z + d, NZ)
        along_z[d] = (other, at(o, p, e, other, c))
    return own, group, same, along_z, at(o, 1 - p, e, z, c)


def enter(group, along_z, across):
    barrier = pltpu.get_barrier_semaphore()
    devices = [entry[-1] for entry in group] + [device for _, device in along_z.values()] + [across]
    for device in devices:
        pl.semaphore_signal(barrier, inc=1, device_id=device, device_id_type=MESH)
    return len(devices)


def send(src, dst, send_sem, recv_sem, device):
    copy = pltpu.make_async_remote_copy(
        src_ref=src, dst_ref=dst, send_sem=send_sem, recv_sem=recv_sem, device_id=device, device_id_type=MESH
    )
    copy.start()
    return copy


def gather_kernel(
    count_ref, tile_mon_hbm, tile_out_hbm, lodf_hbm, flow_hbm, rating_hbm, mon_hbm,
    tiles_ref, gathered_ref, mon_all_ref, rating_all_ref, meta_all_ref,
    tile_mon_ref, tile_out_ref, lodf_ref, flow_ref, tiles_out, flow_out, flow_in, loads, gs, gr, fs, fr, ms, mr, zs, zr, ys, yr,
):
    o, p, e, z, c = position()
    place = e * NX + o
    unit = e * NC + c
    load_flow = pltpu.make_async_copy(flow_hbm, flow_ref, loads.at[0])
    load_lodf = pltpu.make_async_copy(lodf_hbm, lodf_ref, loads.at[1])
    load_mon = pltpu.make_async_copy(mon_hbm, mon_all_ref.at[unit], loads.at[2])
    load_rating = pltpu.make_async_copy(rating_hbm, rating_all_ref.at[unit], loads.at[3])
    words_in = [
        pltpu.make_async_copy(tile_mon_hbm, tile_mon_ref, loads.at[4]),
        pltpu.make_async_copy(tile_out_hbm, tile_out_ref, loads.at[5]),
    ]
    for load in [load_flow, load_lodf, load_mon, load_rating] + words_in:
        load.start()
    own, group, same, along_z, across = peers(o, p, e, z, c)
    signals = enter(group, along_z, across)
    for load in words_in:
        load.wait()
    lane = lax.broadcasted_iota(jnp.int32, (1, S), 1)
    words = jnp.where(lane == 2 * SLOTS, count_ref[0, 0], 0)
    for q in range(SLOTS):
        block = tile_out_ref[0, q]
        across_y = block // NZ
        pair = across_y // 2
        row = (pair * NZ + lax.rem(block, NZ)) * SAME + lax.rem(across_y + pair, 2) * NX + o
        words = jnp.where(lane == q, unit * MB + tile_mon_ref[0, q], words)
        words = jnp.where(lane == SLOTS + q, row, words)
    meta_all_ref[own] = words
    load_flow.wait()
    flow_out[...] = flow_ref[...].astype(F32).reshape(SAME, KC, S)
    flow_in[place] = flow_out[place]
    load_lodf.wait()
    for q in range(0, SLOTS, 2):
        first = jnp.transpose(lodf_ref[q].astype(F32))
        second = jnp.transpose(lodf_ref[q + 1].astype(F32))
        for m in range(G):
            rows = slice(m * KC, (m + 1) * KC)
            tiles_out[m, q * KC : (q + 2) * KC, :] = jnp.concatenate([first[rows], second[rows]], axis=0).astype(BF16)
    tiles_ref[own] = tiles_out[own]
    load_mon.wait()
    load_rating.wait()

    pl.semaphore_wait(pltpu.get_barrier_semaphore(), signals)
    flows = [
        send(flow_out.at[other], flow_in.at[place], fs.at[d], fr.at[d], device)
        for d, (other, device) in enumerate(same)
    ]
    rest = []
    for d, (other, _, _, _, device) in enumerate(group):
        rest.append(send(tiles_out.at[other], tiles_ref.at[own], gs.at[0, d], gr.at[0, d], device))
    for d, (other, _, _, _, device) in enumerate(group):
        rest.append(send(meta_all_ref.at[own], meta_all_ref.at[own], gs.at[1, d], gr.at[1, d], device))
    for d in range(1, 2 * NC):
        other = lax.rem(unit + d, 2 * NC)
        device = at(o, p, other // NC, z, lax.rem(other, NC))
        rest.append(send(mon_all_ref.at[unit], mon_all_ref.at[unit], ms.at[0, d - 1], mr.at[0, d - 1], device))
        rest.append(send(rating_all_ref.at[unit], rating_all_ref.at[unit], ms.at[1, d - 1], mr.at[1, d - 1], device))
    for copy in flows:
        copy.wait()
    mine = p * NZ + z
    gathered_ref[mine] = flow_in[...].reshape(SAME * KC, S).astype(BF16)
    block = gathered_ref.at[mine]
    hops = {}
    for d in (4, 3, 5, 2, 6, 1, 7):
        hops[d] = send(block, block, zs.at[d - 1], zr.at[d - 1], along_z[d][1])
    crossed = [send(block, block, ys.at[0], yr.at[0], across)]
    for d in (1, 7, 2, 6, 3, 5, 4):
        hops[d].wait_recv()
        block = gathered_ref.at[p * NZ + lax.rem(z + NZ - d, NZ)]
        crossed.append(send(block, block, ys.at[d], yr.at[d], across))
    for copy in hops.values():
        copy.wait_send()
    for copy in rest + crossed:
        copy.wait()


def tile_kernel(
    meta_ref, tiles_ref, flow_ref, mon_ref, rating_ref, weights_hbm,
    grad_mon_ref, grad_out_ref,
    from_list, block_list, set_list, weights_ref, load, scaled, column, row_scale, spread, pieces, flows, wide_a, wide_b,
):
    load_weights = pltpu.make_async_copy(weights_hbm, weights_ref, load)
    load_weights.start()
    for u in range(2 * NC):
        for t in range(MB):
            b = u * MB + t
            scale = math.sqrt(LOG2E) / rating_ref[u, t : t + 1, :]
            row_scale[b, :, :] = scale
            turned = jnp.transpose(jnp.broadcast_to(scale, (BLK, BLK)))
            column[b * BLK : (b + 1) * BLK, :] = turned
            scaled[b * BLK : (b + 1) * BLK, :] = turned * mon_ref[u, t * BLK : (t + 1) * BLK, :].astype(F32)
    row_scale[UNITS, :, :] = jnp.zeros((1, BLK), F32)
    scaled[UNITS * BLK :, :] = jnp.zeros((BLK, S), F32)
    grad_mon_ref[...] = jnp.zeros_like(grad_mon_ref)
    grad_out_ref[...] = jnp.zeros_like(grad_out_ref)
    pieces[...] = tiles_ref[...].astype(F32).reshape(G * SLOTS, KC, BLK)
    flows[0:SETS] = flow_ref[...].astype(F32).reshape(SETS, KC, S)
    flows[SETS] = jnp.zeros((KC, S), F32)
    term = lax.broadcasted_iota(jnp.int32, spread.shape, 0)
    lane = lax.broadcasted_iota(jnp.int32, spread.shape, 1)
    spread[...] = jnp.where(lax.rem(term, KC) == lane // S, 1.0, 0.0).astype(BF16)

    def list_member(member, total):
        count = meta_ref[member, 0, 2 * SLOTS]

        def add(q, _):
            from_list[total + q] = member * SLOTS + q
            block_list[total + q] = meta_ref[member, 0, q]
            set_list[total + q] = meta_ref[member, 0, SLOTS + q]
            return 0

        lax.fori_loop(0, count, add, 0)
        return total + count

    total = lax.fori_loop(0, G, list_member, 0)
    for extra in range(3):
        from_list[total + extra] = 0
        block_list[total + extra] = UNITS
        set_list[total + extra] = SETS

    def expand(n, wide):
        piece = pieces[from_list[n]] * row_scale[block_list[n]]
        high = piece.astype(BF16).astype(F32)
        both = jnp.concatenate([high, piece - high], axis=0).astype(BF16)
        wide[...] = lax.dot_general(both, spread[...], (((0,), (0,)), ((), ())), preferred_element_type=F32)

    def work(n, wide):
        row = set_list[n]
        start = pl.multiple_of(block_list[n] * BLK, BLK)
        flow = [flows[row, pl.ds(j, 8, stride=0), :] for j in range(KC)]
        sums = [None] * KC
        for i in range(BLK // 8):
            base = scaled[pl.ds(start + i * 8, 8), :]
            total_m = None
            for j in range(KC):
                factor = wide[i * 8 : (i + 1) * 8, j * S : (j + 1) * S]
                post = base + factor * flow[j]
                square = post * post
                level = jnp.log2(jnp.exp2(square) + math.e)
                slope = (level - LOG2E) * jnp.exp2(square - level) * post
                total_m = slope if total_m is None else total_m + slope
                part = factor * slope
                sums[j] = part if sums[j] is None else sums[j] + part
            grad_mon_ref[pl.ds(start + i * 8, 8), :] += total_m
        grad_out_ref[row] += jnp.concatenate([jnp.sum(v, axis=0, keepdims=True) for v in sums], axis=0)

    expand(0, wide_a)

    def steps(first, count):
        for k in range(0, count, 2):
            expand(first + k + 1, wide_b)
            work(first + k, wide_a)
            expand(first + k + 2, wide_a)
            work(first + k + 1, wide_b)
        return 0

    long = total // UNROLL
    lax.fori_loop(0, long, lambda n, _: steps(n * UNROLL, UNROLL), 0)
    done = long * UNROLL
    lax.fori_loop(0, (total - done + 1) // 2, lambda n, _: steps(done + 2 * n, 2), 0)
    load_weights.wait()
    weight = weights_ref[...] * (4.0 / BLK * math.log(2.0) ** 2)
    grad_mon_ref[0 : UNITS * BLK, :] = grad_mon_ref[0 : UNITS * BLK, :] * column[...] * weight
    grad_out_ref[...] = grad_out_ref[...] * weight[None]


def scatter_kernel(
    mon_ref, flow_ref, grad_mon_ref, grad_out_ref,
    mon_in, y_in, y_sum, z_in, z_sum, last_in,
    gs, gr, fs, fr, zs, zr, ys, yr,
):
    o, p, e, z, c = position()
    own, group, same, along_z, across = peers(o, p, e, z, c)
    place = e * NX + o
    signals = enter(group, along_z, across)
    pl.semaphore_wait(pltpu.get_barrier_semaphore(), signals)

    order = (4, 3, 5, 2, 6, 1, 7, 0)
    crossed = {}
    for d in order:
        there = pl.ds(((1 - p) * NZ + lax.rem(z + d, NZ)) * SAME, SAME)
        crossed[d] = send(flow_ref.at[there], y_in.at[d], ys.at[d], yr.at[d], across)
    group_hops = []
    for d, (other, oo, oe, oc, device) in enumerate(group):
        rows = pl.ds(pl.multiple_of((oe * NC + oc) * MB * BLK + oo * OWN, 8), OWN)
        group_hops.append(send(mon_ref.at[rows], mon_in.at[d], gs.at[d], gr.at[d], device))
    hops = []
    for d in order:
        crossed[d].wait()
        here = pl.ds((p * NZ + lax.rem(z + d, NZ)) * SAME, SAME)
        y_sum[d] = flow_ref[here] + y_in[d]
        if d > 0:
            hops.append(send(y_sum.at[d], z_in.at[d - 1], zs.at[d - 1], zr.at[d - 1], along_z[d][1]))
    for copy in hops:
        copy.wait()
    total = y_sum[0]
    for d in range(NZ - 1):
        total = total + z_in[d]
    z_sum[...] = total
    last_in[place] = z_sum[place]
    hops = [
        send(z_sum.at[other], last_in.at[place], fs.at[d], fr.at[d], device)
        for d, (other, device) in enumerate(same)
    ]
    for copy in group_hops:
        copy.wait()
    rows = pl.ds(pl.multiple_of((e * NC + c) * MB * BLK + o * OWN, 8), OWN)
    total = mon_ref[rows, :]
    for d in range(G - 1):
        total = total + mon_in[d]
    grad_mon_ref[...] = total
    for copy in hops:
        copy.wait()
    for m in range(SAME):
        grad_out_ref[m * KC : (m + 1) * KC, :] = last_in[m]


def vmem(count):
    return [pl.BlockSpec(memory_space=pltpu.VMEM)] * count


DMA = pltpu.SemaphoreType.DMA


def local(mon_flow, out_flow, rating, weights, lodf, tile_mon, tile_out, tile_count):
    inputs = [
        tile_mon[0], tile_out[0],
        lodf[0, 0], out_flow[0], rating.reshape(MB, BLK), mon_flow, weights.reshape(1, S),
    ]
    inputs = [pltpu.with_memory_space_constraint(x, pltpu.HBM) for x in inputs]
    tiles, gathered, mon_all, ratings, meta_all = pl.pallas_call(
        gather_kernel,
        out_shape=(
            jax.ShapeDtypeStruct((G, SLOTS * KC, BLK), BF16),
            jax.ShapeDtypeStruct((NP * NZ, SAME * KC, S), BF16),
            jax.ShapeDtypeStruct((2 * NC, MB * BLK, S), BF16),
            jax.ShapeDtypeStruct((2 * NC, MB, BLK), F32),
            jax.ShapeDtypeStruct((G, 1, S), jnp.int32),
        ),
        in_specs=[pl.BlockSpec(memory_space=pltpu.SMEM)] + [pl.BlockSpec(memory_space=pltpu.HBM)] * 6,
        out_specs=tuple(vmem(5)),
        scratch_shapes=[
            pltpu.SMEM((1, SLOTS), jnp.int32),
            pltpu.SMEM((1, SLOTS), jnp.int32),
            pltpu.VMEM((SLOTS, BLK, BLK), BF16),
            pltpu.VMEM((SAME * KC, S), BF16),
            pltpu.VMEM((G, SLOTS * KC, BLK), BF16),
            pltpu.VMEM((SAME, KC, S), F32),
            pltpu.VMEM((SAME, KC, S), F32),
            DMA((6,)), DMA((2, G - 1)), DMA((2, G - 1)), DMA((SAME - 1,)), DMA((SAME - 1,)),
            DMA((2, 2 * NC - 1)), DMA((2, 2 * NC - 1)), DMA((NZ - 1,)), DMA((NZ - 1,)), DMA((NZ,)), DMA((NZ,)),
        ],
        compiler_params=pltpu.CompilerParams(collective_id=0, has_side_effects=True, vmem_limit_bytes=VMEM_BYTES),
        name="gather",
    )(tile_count, *inputs[:6])

    part_mon, part_out = pl.pallas_call(
        tile_kernel,
        out_shape=(
            jax.ShapeDtypeStruct(((UNITS + 1) * BLK, S), F32),
            jax.ShapeDtypeStruct((SETS + 1, KC, S), F32),
        ),
        in_specs=[pl.BlockSpec(memory_space=pltpu.SMEM)] + vmem(4) + [pl.BlockSpec(memory_space=pltpu.HBM)],
        out_specs=tuple(vmem(2)),
        scratch_shapes=[
            pltpu.SMEM((G * SLOTS + 8,), jnp.int32),
            pltpu.SMEM((G * SLOTS + 8,), jnp.int32),
            pltpu.SMEM((G * SLOTS + 8,), jnp.int32),
            pltpu.VMEM((1, S), F32),
            DMA,
            pltpu.VMEM(((UNITS + 1) * BLK, S), F32),
            pltpu.VMEM((UNITS * BLK, S), F32),
            pltpu.VMEM((UNITS + 1, 1, BLK), F32),
            pltpu.VMEM((2 * KC, KC * S), BF16),
            pltpu.VMEM((G * SLOTS, KC, BLK), F32),
            pltpu.VMEM((SETS + 1, KC, S), F32),
            pltpu.VMEM((BLK, KC * S), F32),
            pltpu.VMEM((BLK, KC * S), F32),
        ],
        compiler_params=pltpu.CompilerParams(vmem_limit_bytes=VMEM_BYTES),
        name="tiles",
    )(meta_all, tiles, gathered, mon_all, ratings, inputs[6])

    grad_mon, grad_out = pl.pallas_call(
        scatter_kernel,
        out_shape=(
            jax.ShapeDtypeStruct((OWN, S), F32),
            jax.ShapeDtypeStruct((SAME * KC, S), F32),
        ),
        in_specs=vmem(2),
        out_specs=tuple(vmem(2)),
        scratch_shapes=[
            pltpu.VMEM((G - 1, OWN, S), F32),
            pltpu.VMEM((NZ, SAME, KC, S), F32),
            pltpu.VMEM((NZ, SAME, KC, S), F32),
            pltpu.VMEM((NZ - 1, SAME, KC, S), F32),
            pltpu.VMEM((SAME, KC, S), F32),
            pltpu.VMEM((SAME, KC, S), F32),
            DMA((G - 1,)), DMA((G - 1,)), DMA((SAME - 1,)), DMA((SAME - 1,)),
            DMA((NZ - 1,)), DMA((NZ - 1,)), DMA((NZ,)), DMA((NZ,)),
        ],
        compiler_params=pltpu.CompilerParams(
            collective_id=1, has_side_effects=True, vmem_limit_bytes=VMEM_BYTES
        ),
        name="scatter",
    )(part_mon, part_out)
    return grad_mon, grad_out[None]


def solution(mesh):
    in_specs = (
        P("mon", None),
        P("out", "mon", None),
        P("mon"),
        P(),
        P("mon", "out", None, None, None),
        P("mon", "out", None),
        P("mon", "out", None),
        P("mon", "out"),
    )
    out_specs = (P(("mon", "out"), None), P("out", "mon", None))
    return jax.shard_map(local, mesh=mesh, in_specs=in_specs, out_specs=out_specs, check_vma=False)
```

```python
import functools
import math

import jax
import jax.numpy as jnp
from jax import lax
from jax.experimental import pallas as pl
from jax.experimental.pallas import tpu as pltpu
from jax.sharding import PartitionSpec as P

MESH = pl.DeviceIdType.MESH
NX, NY, NZ, NC = 4, 4, 8, 2
NP = NY // 2
SAME = 2 * NX
G = SAME * NC
BLK = 128
S = 128
SLOTS = 8
KC = BLK // G
MB = 3
UNROLL = 8
UNITS = 2 * NC * MB
SETS = NP * NZ * SAME
OWN = MB * BLK // NX
LOG2E = math.log2(math.e)
VMEM_BYTES = 16 << 20
F32 = jnp.float32
BF16 = jnp.bfloat16


def position():
    i = lax.axis_index("mon")
    o = lax.axis_index("out")
    c = lax.rem(i, NC)
    z = lax.rem(i // NC, NZ)
    y = i // (NC * NZ)
    p = y // 2
    return o, p, lax.rem(y + p, 2), z, c


def at(o, p, e, z, c):
    y = 2 * p + lax.rem(e + p, 2)
    return ((y * NZ + z) * NC + c, o)


def peers(o, p, e, z, c):
    own = (c * 2 + e) * NX + o
    group = []
    for d in range(1, G):
        other = lax.rem(own + d, G)
        oo, oe, oc = lax.rem(other, NX), lax.rem(other // NX, 2), other // SAME
        group.append((other, oo, oe, oc, at(oo, p, oe, z, oc)))
    same = []
    for d in range(1, SAME):
        other = lax.rem(e * NX + o + d, SAME)
        same.append((other, at(lax.rem(other, NX), p, other // NX, z, c)))
    along_z = {}
    for d in range(1, NZ):
        other = lax.rem(z + d, NZ)
        along_z[d] = (other, at(o, p, e, other, c))
    return own, group, same, along_z, at(o, 1 - p, e, z, c)


def enter(group, along_z, across):
    barrier = pltpu.get_barrier_semaphore()
    devices = [entry[-1] for entry in group] + [device for _, device in along_z.values()] + [across]
    for device in devices:
        pl.semaphore_signal(barrier, inc=1, device_id=device, device_id_type=MESH)
    return len(devices)


def send(src, dst, send_sem, recv_sem, device):
    copy = pltpu.make_async_remote_copy(
        src_ref=src, dst_ref=dst, send_sem=send_sem, recv_sem=recv_sem, device_id=device, device_id_type=MESH
    )
    copy.start()
    return copy


def gather_kernel(
    count_ref, tile_mon_hbm, tile_out_hbm, lodf_hbm, flow_hbm, rating_hbm, mon_hbm,
    tiles_ref, gathered_ref, mon_all_ref, rating_all_ref, meta_all_ref,
    tile_mon_ref, tile_out_ref, lodf_ref, flow_ref, tiles_out, flow_out, flow_in, loads, gs, gr, fs, fr, ms, mr, zs, zr, ys, yr,
):
    o, p, e, z, c = position()
    place = e * NX + o
    unit = e * NC + c
    load_flow = pltpu.make_async_copy(flow_hbm, flow_ref, loads.at[0])
    load_lodf = pltpu.make_async_copy(lodf_hbm, lodf_ref, loads.at[1])
    load_mon = pltpu.make_async_copy(mon_hbm, mon_all_ref.at[unit], loads.at[2])
    load_rating = pltpu.make_async_copy(rating_hbm, rating_all_ref.at[unit], loads.at[3])
    words_in = [
        pltpu.make_async_copy(tile_mon_hbm, tile_mon_ref, loads.at[4]),
        pltpu.make_async_copy(tile_out_hbm, tile_out_ref, loads.at[5]),
    ]
    for load in [load_flow, load_lodf, load_mon, load_rating] + words_in:
        load.start()
    own, group, same, along_z, across = peers(o, p, e, z, c)
    signals = enter(group, along_z, across)
    for load in words_in:
        load.wait()
    lane = lax.broadcasted_iota(jnp.int32, (1, S), 1)
    words = jnp.where(lane == 2 * SLOTS, count_ref[0, 0], 0)
    for q in range(SLOTS):
        block = tile_out_ref[0, q]
        across_y = block // NZ
        pair = across_y // 2
        row = (pair * NZ + lax.rem(block, NZ)) * SAME + lax.rem(across_y + pair, 2) * NX + o
        words = jnp.where(lane == q, unit * MB + tile_mon_ref[0, q], words)
        words = jnp.where(lane == SLOTS + q, row, words)
    meta_all_ref[own] = words
    load_flow.wait()
    flow_out[...] = flow_ref[...].astype(F32).reshape(SAME, KC, S)
    flow_in[place] = flow_out[place]
    load_lodf.wait()
    for q in range(0, SLOTS, 2):
        first = jnp.transpose(lodf_ref[q].astype(F32))
        second = jnp.transpose(lodf_ref[q + 1].astype(F32))
        for m in range(G):
            rows = slice(m * KC, (m + 1) * KC)
            tiles_out[m, q * KC : (q + 2) * KC, :] = jnp.concatenate([first[rows], second[rows]], axis=0).astype(BF16)
    tiles_ref[own] = tiles_out[own]
    load_mon.wait()
    load_rating.wait()

    pl.semaphore_wait(pltpu.get_barrier_semaphore(), signals)
    flows = [
        send(flow_out.at[other], flow_in.at[place], fs.at[d], fr.at[d], device)
        for d, (other, device) in enumerate(same)
    ]
    rest = []
    for d, (other, _, _, _, device) in enumerate(group):
        rest.append(send(tiles_out.at[other], tiles_ref.at[own], gs.at[0, d], gr.at[0, d], device))
    for d, (other, _, _, _, device) in enumerate(group):
        rest.append(send(meta_all_ref.at[own], meta_all_ref.at[own], gs.at[1, d], gr.at[1, d], device))
    for d in range(1, 2 * NC):
        other = lax.rem(unit + d, 2 * NC)
        device = at(o, p, other // NC, z, lax.rem(other, NC))
        rest.append(send(mon_all_ref.at[unit], mon_all_ref.at[unit], ms.at[0, d - 1], mr.at[0, d - 1], device))
        rest.append(send(rating_all_ref.at[unit], rating_all_ref.at[unit], ms.at[1, d - 1], mr.at[1, d - 1], device))
    for copy in flows:
        copy.wait()
    mine = p * NZ + z
    gathered_ref[mine] = flow_in[...].reshape(SAME * KC, S).astype(BF16)
    block = gathered_ref.at[mine]
    hops = {}
    for d in (4, 3, 5, 2, 6, 1, 7):
        hops[d] = send(block, block, zs.at[d - 1], zr.at[d - 1], along_z[d][1])
    crossed = [send(block, block, ys.at[0], yr.at[0], across)]
    for d in (1, 7, 2, 6, 3, 5, 4):
        hops[d].wait_recv()
        block = gathered_ref.at[p * NZ + lax.rem(z + NZ - d, NZ)]
        crossed.append(send(block, block, ys.at[d], yr.at[d], across))
    for copy in hops.values():
        copy.wait_send()
    for copy in rest + crossed:
        copy.wait()


def tile_kernel(
    words_ref, tiles_ref, flow_ref, mon_ref, rating_ref, weights_hbm,
    grad_mon_ref, grad_out_ref,
    meta_ref, from_list, block_list, set_list, weights_ref, load, load_words, scaled, column, row_scale, spread, pieces, flows, wide_a, wide_b,
):
    load_weights = pltpu.make_async_copy(weights_hbm, weights_ref, load)
    load_weights.start()
    words = pltpu.make_async_copy(words_ref, meta_ref, load_words)
    words.start()
    for u in range(2 * NC):
        for t in range(MB):
            b = u * MB + t
            scale = math.sqrt(LOG2E) / rating_ref[u, t : t + 1, :]
            row_scale[b, :, :] = scale
            turned = jnp.transpose(jnp.broadcast_to(scale, (BLK, BLK)))
            column[b * BLK : (b + 1) * BLK, :] = turned
            scaled[b * BLK : (b + 1) * BLK, :] = turned * mon_ref[u, t * BLK : (t + 1) * BLK, :].astype(F32)
    row_scale[UNITS, :, :] = jnp.zeros((1, BLK), F32)
    scaled[UNITS * BLK :, :] = jnp.zeros((BLK, S), F32)
    grad_mon_ref[...] = jnp.zeros_like(grad_mon_ref)
    grad_out_ref[...] = jnp.zeros_like(grad_out_ref)
    pieces[...] = tiles_ref[...].astype(F32).reshape(G * SLOTS, KC, BLK)
    flows[0:SETS] = flow_ref[...].astype(F32).reshape(SETS, KC, S)
    flows[SETS] = jnp.zeros((KC, S), F32)
    term = lax.broadcasted_iota(jnp.int32, spread.shape, 0)
    lane = lax.broadcasted_iota(jnp.int32, spread.shape, 1)
    spread[...] = jnp.where(lax.rem(term, KC) == lane // S, 1.0, 0.0).astype(BF16)

    words.wait()

    def list_member(member, total):
        count = meta_ref[member, 0, 2 * SLOTS]

        def add(q, _):
            from_list[total + q] = member * SLOTS + q
            block_list[total + q] = meta_ref[member, 0, q]
            set_list[total + q] = meta_ref[member, 0, SLOTS + q]
            return 0

        lax.fori_loop(0, count, add, 0)
        return total + count

    total = lax.fori_loop(0, G, list_member, 0)
    for extra in range(3):
        from_list[total + extra] = 0
        block_list[total + extra] = UNITS
        set_list[total + extra] = SETS

    def expand(n, wide):
        piece = pieces[from_list[n]] * row_scale[block_list[n]]
        high = piece.astype(BF16).astype(F32)
        both = jnp.concatenate([high, piece - high], axis=0).astype(BF16)
        wide[...] = lax.dot_general(both, spread[...], (((0,), (0,)), ((), ())), preferred_element_type=F32)

    def work(n, wide):
        row = set_list[n]
        start = pl.multiple_of(block_list[n] * BLK, BLK)
        flow = [flows[row, pl.ds(j, 8, stride=0), :] for j in range(KC)]
        sums = [None] * KC
        for i in range(BLK // 8):
            base = scaled[pl.ds(start + i * 8, 8), :]
            total_m = None
            for j in range(KC):
                factor = wide[i * 8 : (i + 1) * 8, j * S : (j + 1) * S]
                post = base + factor * flow[j]
                square = post * post
                level = jnp.log2(jnp.exp2(square) + math.e)
                slope = (level - LOG2E) * jnp.exp2(square - level) * post
                total_m = slope if total_m is None else total_m + slope
                part = factor * slope
                sums[j] = part if sums[j] is None else sums[j] + part
            grad_mon_ref[pl.ds(start + i * 8, 8), :] += total_m
        grad_out_ref[row] += jnp.concatenate([jnp.sum(v, axis=0, keepdims=True) for v in sums], axis=0)

    expand(0, wide_a)

    def steps(first, count):
        for k in range(0, count, 2):
            expand(first + k + 1, wide_b)
            work(first + k, wide_a)
            expand(first + k + 2, wide_a)
            work(first + k + 1, wide_b)
        return 0

    long = total // UNROLL
    lax.fori_loop(0, long, lambda n, _: steps(n * UNROLL, UNROLL), 0)
    done = long * UNROLL
    lax.fori_loop(0, (total - done + 1) // 2, lambda n, _: steps(done + 2 * n, 2), 0)
    load_weights.wait()
    weight = weights_ref[...] * (4.0 / BLK * math.log(2.0) ** 2)
    grad_mon_ref[0 : UNITS * BLK, :] = grad_mon_ref[0 : UNITS * BLK, :] * column[...] * weight
    grad_out_ref[...] = grad_out_ref[...] * weight[None]


def scatter_kernel(
    mon_ref, flow_ref, grad_mon_ref, grad_out_ref,
    mon_in, y_in, y_sum, z_in, z_sum, last_in,
    gs, gr, fs, fr, zs, zr, ys, yr,
):
    o, p, e, z, c = position()
    own, group, same, along_z, across = peers(o, p, e, z, c)
    place = e * NX + o
    signals = enter(group, along_z, across)
    pl.semaphore_wait(pltpu.get_barrier_semaphore(), signals)

    order = (4, 3, 5, 2, 6, 1, 7, 0)
    crossed = {}
    for d in order:
        there = pl.ds(((1 - p) * NZ + lax.rem(z + d, NZ)) * SAME, SAME)
        crossed[d] = send(flow_ref.at[there], y_in.at[d], ys.at[d], yr.at[d], across)
    group_hops = []
    for d, (other, oo, oe, oc, device) in enumerate(group):
        rows = pl.ds(pl.multiple_of((oe * NC + oc) * MB * BLK + oo * OWN, 8), OWN)
        group_hops.append(send(mon_ref.at[rows], mon_in.at[d], gs.at[d], gr.at[d], device))
    hops = []
    for d in order:
        crossed[d].wait()
        here = pl.ds((p * NZ + lax.rem(z + d, NZ)) * SAME, SAME)
        y_sum[d] = flow_ref[here] + y_in[d]
        if d > 0:
            hops.append(send(y_sum.at[d], z_in.at[d - 1], zs.at[d - 1], zr.at[d - 1], along_z[d][1]))
    for copy in hops:
        copy.wait()
    total = y_sum[0]
    for d in range(NZ - 1):
        total = total + z_in[d]
    z_sum[...] = total
    last_in[place] = z_sum[place]
    hops = [
        send(z_sum.at[other], last_in.at[place], fs.at[d], fr.at[d], device)
        for d, (other, device) in enumerate(same)
    ]
    for copy in group_hops:
        copy.wait()
    rows = pl.ds(pl.multiple_of((e * NC + c) * MB * BLK + o * OWN, 8), OWN)
    total = mon_ref[rows, :]
    for d in range(G - 1):
        total = total + mon_in[d]
    grad_mon_ref[...] = total
    for copy in hops:
        copy.wait()
    for m in range(SAME):
        grad_out_ref[m * KC : (m + 1) * KC, :] = last_in[m]


def store_kernel(mon_ref, flow_ref, mon_hbm, flow_hbm, sems):
    stores = [
        pltpu.make_async_copy(mon_ref, mon_hbm, sems.at[0]),
        pltpu.make_async_copy(flow_ref, flow_hbm, sems.at[1]),
    ]
    for store in stores:
        store.start()
    for store in stores:
        store.wait()


def vmem(count):
    return [pl.BlockSpec(memory_space=pltpu.VMEM)] * count


DMA = pltpu.SemaphoreType.DMA


def local(mon_flow, out_flow, rating, weights, lodf, tile_mon, tile_out, tile_count):
    inputs = [
        tile_mon[0], tile_out[0],
        lodf[0, 0], out_flow[0], rating.reshape(MB, BLK), mon_flow, weights.reshape(1, S),
    ]
    inputs = [pltpu.with_memory_space_constraint(x, pltpu.HBM) for x in inputs]
    tiles, gathered, mon_all, ratings, meta_all = pl.pallas_call(
        gather_kernel,
        out_shape=(
            jax.ShapeDtypeStruct((G, SLOTS * KC, BLK), BF16),
            jax.ShapeDtypeStruct((NP * NZ, SAME * KC, S), BF16),
            jax.ShapeDtypeStruct((2 * NC, MB * BLK, S), BF16),
            jax.ShapeDtypeStruct((2 * NC, MB, BLK), F32),
            jax.ShapeDtypeStruct((G, 1, S), jnp.int32),
        ),
        in_specs=[pl.BlockSpec(memory_space=pltpu.SMEM)] + [pl.BlockSpec(memory_space=pltpu.HBM)] * 6,
        out_specs=tuple(vmem(5)),
        scratch_shapes=[
            pltpu.SMEM((1, SLOTS), jnp.int32),
            pltpu.SMEM((1, SLOTS), jnp.int32),
            pltpu.VMEM((SLOTS, BLK, BLK), BF16),
            pltpu.VMEM((SAME * KC, S), BF16),
            pltpu.VMEM((G, SLOTS * KC, BLK), BF16),
            pltpu.VMEM((SAME, KC, S), F32),
            pltpu.VMEM((SAME, KC, S), F32),
            DMA((6,)), DMA((2, G - 1)), DMA((2, G - 1)), DMA((SAME - 1,)), DMA((SAME - 1,)),
            DMA((2, 2 * NC - 1)), DMA((2, 2 * NC - 1)), DMA((NZ - 1,)), DMA((NZ - 1,)), DMA((NZ,)), DMA((NZ,)),
        ],
        compiler_params=pltpu.CompilerParams(collective_id=0, has_side_effects=True, vmem_limit_bytes=VMEM_BYTES),
        name="gather",
    )(tile_count, *inputs[:6])

    part_mon, part_out = pl.pallas_call(
        tile_kernel,
        out_shape=(
            jax.ShapeDtypeStruct(((UNITS + 1) * BLK, S), F32),
            jax.ShapeDtypeStruct((SETS + 1, KC, S), F32),
        ),
        in_specs=vmem(5) + [pl.BlockSpec(memory_space=pltpu.HBM)],
        out_specs=tuple(vmem(2)),
        scratch_shapes=[
            pltpu.SMEM((G, 1, S), jnp.int32),
            pltpu.SMEM((G * SLOTS + 8,), jnp.int32),
            pltpu.SMEM((G * SLOTS + 8,), jnp.int32),
            pltpu.SMEM((G * SLOTS + 8,), jnp.int32),
            pltpu.VMEM((1, S), F32),
            DMA,
            DMA,
            pltpu.VMEM(((UNITS + 1) * BLK, S), F32),
            pltpu.VMEM((UNITS * BLK, S), F32),
            pltpu.VMEM((UNITS + 1, 1, BLK), F32),
            pltpu.VMEM((2 * KC, KC * S), BF16),
            pltpu.VMEM((G * SLOTS, KC, BLK), F32),
            pltpu.VMEM((SETS + 1, KC, S), F32),
            pltpu.VMEM((BLK, KC * S), F32),
            pltpu.VMEM((BLK, KC * S), F32),
        ],
        compiler_params=pltpu.CompilerParams(vmem_limit_bytes=VMEM_BYTES),
        name="tiles",
    )(meta_all, tiles, gathered, mon_all, ratings, inputs[6])

    grad_mon, grad_out = pl.pallas_call(
        scatter_kernel,
        out_shape=(
            jax.ShapeDtypeStruct((OWN, S), F32),
            jax.ShapeDtypeStruct((SAME * KC, S), F32),
        ),
        in_specs=vmem(2),
        out_specs=tuple(vmem(2)),
        scratch_shapes=[
            pltpu.VMEM((G - 1, OWN, S), F32),
            pltpu.VMEM((NZ, SAME, KC, S), F32),
            pltpu.VMEM((NZ, SAME, KC, S), F32),
            pltpu.VMEM((NZ - 1, SAME, KC, S), F32),
            pltpu.VMEM((SAME, KC, S), F32),
            pltpu.VMEM((SAME, KC, S), F32),
            DMA((G - 1,)), DMA((G - 1,)), DMA((SAME - 1,)), DMA((SAME - 1,)),
            DMA((NZ - 1,)), DMA((NZ - 1,)), DMA((NZ,)), DMA((NZ,)),
        ],
        compiler_params=pltpu.CompilerParams(
            collective_id=1, has_side_effects=True, vmem_limit_bytes=VMEM_BYTES
        ),
        name="scatter",
    )(part_mon, part_out)
    grad_mon, grad_out = pl.pallas_call(
        store_kernel,
        out_shape=(
            jax.ShapeDtypeStruct((OWN, S), F32),
            jax.ShapeDtypeStruct((SAME * KC, S), F32),
        ),
        in_specs=vmem(2),
        out_specs=tuple([pl.BlockSpec(memory_space=pltpu.HBM)] * 2),
        scratch_shapes=[DMA((2,))],
        compiler_params=pltpu.CompilerParams(vmem_limit_bytes=VMEM_BYTES),
        name="store",
    )(grad_mon, grad_out)
    return grad_mon, grad_out[None]


def solution(mesh):
    in_specs = (
        P("mon", None),
        P("out", "mon", None),
        P("mon"),
        P(),
        P("mon", "out", None, None, None),
        P("mon", "out", None),
        P("mon", "out", None),
        P("mon", "out"),
    )
    out_specs = (P(("mon", "out"), None), P("out", "mon", None))
    return jax.shard_map(local, mesh=mesh, in_specs=in_specs, out_specs=out_specs, check_vma=False)
```

```python
import functools
import math

import jax
import jax.numpy as jnp
from jax import lax
from jax.experimental import pallas as pl
from jax.experimental.pallas import tpu as pltpu
from jax.sharding import PartitionSpec as P

MESH = pl.DeviceIdType.MESH
NX, NY, NZ, NC = 4, 4, 8, 2
NP = NY // 2
SAME = 2 * NX
G = SAME * NC
BLK = 128
S = 128
SLOTS = 8
KC = BLK // G
MB = 3
UNROLL = 8
UNITS = 2 * NC * MB
SETS = NP * NZ * SAME
OWN = MB * BLK // NX
LOG2E = math.log2(math.e)
VMEM_BYTES = 16 << 20
F32 = jnp.float32
BF16 = jnp.bfloat16


def low(value, size):
    return value & (size - 1)


def high(value, size):
    return value >> (size.bit_length() - 1)


def position():
    i = lax.axis_index("mon")
    o = lax.axis_index("out")
    c = low(i, NC)
    z = low(high(i, NC), NZ)
    y = high(i, NC * NZ)
    p = high(y, 2)
    return o, p, low(y + p, 2), z, c


def at(o, p, e, z, c):
    y = 2 * p + low(e + p, 2)
    return ((y * NZ + z) * NC + c, o)


def peers(o, p, e, z, c):
    own = (c * 2 + e) * NX + o
    group = []
    for d in range(1, G):
        other = low(own + d, G)
        oo, oe, oc = low(other, NX), low(high(other, NX), 2), high(other, SAME)
        group.append((other, oo, oe, oc, at(oo, p, oe, z, oc)))
    same = []
    for d in range(1, SAME):
        other = low(e * NX + o + d, SAME)
        same.append((other, at(low(other, NX), p, high(other, NX), z, c)))
    along_z = {}
    for d in range(1, NZ):
        other = low(z + d, NZ)
        along_z[d] = (other, at(o, p, e, other, c))
    return own, group, same, along_z, at(o, 1 - p, e, z, c)


def enter(group, along_z, across):
    barrier = pltpu.get_barrier_semaphore()
    devices = [entry[-1] for entry in group] + [device for _, device in along_z.values()] + [across]
    for device in devices:
        pl.semaphore_signal(barrier, inc=1, device_id=device, device_id_type=MESH)
    return len(devices)


def send(src, dst, send_sem, recv_sem, device):
    copy = pltpu.make_async_remote_copy(
        src_ref=src, dst_ref=dst, send_sem=send_sem, recv_sem=recv_sem, device_id=device, device_id_type=MESH
    )
    copy.start()
    return copy


def gather_kernel(
    count_ref, tile_mon_hbm, tile_out_hbm, lodf_hbm, flow_hbm, rating_hbm, mon_hbm,
    tiles_ref, gathered_ref, mon_all_ref, rating_all_ref, meta_all_ref,
    tile_mon_ref, tile_out_ref, lodf_ref, flow_ref, tiles_out, flow_out, flow_in, loads, gs, gr, fs, fr, ms, mr, zs, zr, ys, yr,
):
    o, p, e, z, c = position()
    place = e * NX + o
    unit = e * NC + c
    load_flow = pltpu.make_async_copy(flow_hbm, flow_ref, loads.at[0])
    load_lodf = pltpu.make_async_copy(lodf_hbm, lodf_ref, loads.at[1])
    load_mon = pltpu.make_async_copy(mon_hbm, mon_all_ref.at[unit], loads.at[2])
    load_rating = pltpu.make_async_copy(rating_hbm, rating_all_ref.at[unit], loads.at[3])
    words_in = [
        pltpu.make_async_copy(tile_mon_hbm, tile_mon_ref, loads.at[4]),
        pltpu.make_async_copy(tile_out_hbm, tile_out_ref, loads.at[5]),
    ]
    for load in [load_flow, load_lodf, load_mon, load_rating] + words_in:
        load.start()
    own, group, same, along_z, across = peers(o, p, e, z, c)
    signals = enter(group, along_z, across)
    for load in words_in:
        load.wait()
    lane = lax.broadcasted_iota(jnp.int32, (1, S), 1)
    words = jnp.where(lane == 2 * SLOTS, count_ref[0, 0], 0)
    for q in range(SLOTS):
        block = tile_out_ref[0, q]
        across_y = block // NZ
        pair = across_y // 2
        row = (pair * NZ + lax.rem(block, NZ)) * SAME + lax.rem(across_y + pair, 2) * NX + o
        words = jnp.where(lane == q, unit * MB + tile_mon_ref[0, q], words)
        words = jnp.where(lane == SLOTS + q, row, words)
    meta_all_ref[own] = words
    load_flow.wait()
    flow_out[...] = flow_ref[...].astype(F32).reshape(SAME, KC, S)
    flow_in[place] = flow_out[place]
    load_lodf.wait()
    for q in range(0, SLOTS, 2):
        first = jnp.transpose(lodf_ref[q].astype(F32))
        second = jnp.transpose(lodf_ref[q + 1].astype(F32))
        for m in range(G):
            rows = slice(m * KC, (m + 1) * KC)
            tiles_out[m, q * KC : (q + 2) * KC, :] = jnp.concatenate([first[rows], second[rows]], axis=0).astype(BF16)
    tiles_ref[own] = tiles_out[own]
    load_mon.wait()
    load_rating.wait()

    pl.semaphore_wait(pltpu.get_barrier_semaphore(), signals)
    flows = [
        send(flow_out.at[other], flow_in.at[place], fs.at[d], fr.at[d], device)
        for d, (other, device) in enumerate(same)
    ]
    rest = []
    for d, (other, _, _, _, device) in enumerate(group):
        rest.append(send(tiles_out.at[other], tiles_ref.at[own], gs.at[0, d], gr.at[0, d], device))
    for d, (other, _, _, _, device) in enumerate(group):
        rest.append(send(meta_all_ref.at[own], meta_all_ref.at[own], gs.at[1, d], gr.at[1, d], device))
    for d in range(1, 2 * NC):
        other = low(unit + d, 2 * NC)
        device = at(o, p, high(other, NC), z, low(other, NC))
        rest.append(send(mon_all_ref.at[unit], mon_all_ref.at[unit], ms.at[0, d - 1], mr.at[0, d - 1], device))
        rest.append(send(rating_all_ref.at[unit], rating_all_ref.at[unit], ms.at[1, d - 1], mr.at[1, d - 1], device))
    for copy in flows:
        copy.wait()
    mine = p * NZ + z
    gathered_ref[mine] = flow_in[...].reshape(SAME * KC, S).astype(BF16)
    block = gathered_ref.at[mine]
    hops = {}
    for d in (4, 3, 5, 2, 6, 1, 7):
        hops[d] = send(block, block, zs.at[d - 1], zr.at[d - 1], along_z[d][1])
    crossed = [send(block, block, ys.at[0], yr.at[0], across)]
    for d in (1, 7, 2, 6, 3, 5, 4):
        hops[d].wait_recv()
        block = gathered_ref.at[p * NZ + low(z + NZ - d, NZ)]
        crossed.append(send(block, block, ys.at[d], yr.at[d], across))
    for copy in hops.values():
        copy.wait_send()
    for copy in rest + crossed:
        copy.wait()


def tile_kernel(
    words_ref, tiles_ref, flow_ref, mon_ref, rating_ref, weights_hbm,
    grad_mon_ref, grad_out_ref,
    meta_ref, from_list, block_list, set_list, weights_ref, load, load_words, scaled, column, row_scale, spread, pieces, flows, wide_a, wide_b,
):
    load_weights = pltpu.make_async_copy(weights_hbm, weights_ref, load)
    load_weights.start()
    words = pltpu.make_async_copy(words_ref, meta_ref, load_words)
    words.start()
    for u in range(2 * NC):
        for t in range(MB):
            b = u * MB + t
            scale = math.sqrt(LOG2E) / rating_ref[u, t : t + 1, :]
            row_scale[b, :, :] = scale
            turned = jnp.transpose(jnp.broadcast_to(scale, (BLK, BLK)))
            column[b * BLK : (b + 1) * BLK, :] = turned
            scaled[b * BLK : (b + 1) * BLK, :] = turned * mon_ref[u, t * BLK : (t + 1) * BLK, :].astype(F32)
    row_scale[UNITS, :, :] = jnp.zeros((1, BLK), F32)
    scaled[UNITS * BLK :, :] = jnp.zeros((BLK, S), F32)
    grad_mon_ref[...] = jnp.zeros_like(grad_mon_ref)
    grad_out_ref[...] = jnp.zeros_like(grad_out_ref)
    pieces[...] = tiles_ref[...].astype(F32).reshape(G * SLOTS, KC, BLK)
    flows[0:SETS] = flow_ref[...].astype(F32).reshape(SETS, KC, S)
    flows[SETS] = jnp.zeros((KC, S), F32)
    term = lax.broadcasted_iota(jnp.int32, spread.shape, 0)
    lane = lax.broadcasted_iota(jnp.int32, spread.shape, 1)
    spread[...] = jnp.where(lax.rem(term, KC) == lane // S, 1.0, 0.0).astype(BF16)

    words.wait()

    def list_member(member, total):
        count = meta_ref[member, 0, 2 * SLOTS]

        def add(q, _):
            from_list[total + q] = member * SLOTS + q
            block_list[total + q] = meta_ref[member, 0, q]
            set_list[total + q] = meta_ref[member, 0, SLOTS + q]
            return 0

        lax.fori_loop(0, count, add, 0)
        return total + count

    total = lax.fori_loop(0, G, list_member, 0)
    for extra in range(3):
        from_list[total + extra] = 0
        block_list[total + extra] = UNITS
        set_list[total + extra] = SETS

    def expand(n, wide):
        piece = pieces[from_list[n]] * row_scale[block_list[n]]
        high = piece.astype(BF16).astype(F32)
        both = jnp.concatenate([high, piece - high], axis=0).astype(BF16)
        wide[...] = lax.dot_general(both, spread[...], (((0,), (0,)), ((), ())), preferred_element_type=F32)

    def work(n, wide):
        row = set_list[n]
        start = pl.multiple_of(block_list[n] * BLK, BLK)
        flow = [flows[row, pl.ds(j, 8, stride=0), :] for j in range(KC)]
        sums = [None] * KC
        for i in range(BLK // 8):
            base = scaled[pl.ds(start + i * 8, 8), :]
            total_m = None
            for j in range(KC):
                factor = wide[i * 8 : (i + 1) * 8, j * S : (j + 1) * S]
                post = base + factor * flow[j]
                square = post * post
                level = jnp.log2(jnp.exp2(square) + math.e)
                slope = (level - LOG2E) * jnp.exp2(square - level) * post
                total_m = slope if total_m is None else total_m + slope
                part = factor * slope
                sums[j] = part if sums[j] is None else sums[j] + part
            grad_mon_ref[pl.ds(start + i * 8, 8), :] += total_m
        grad_out_ref[row] += jnp.concatenate([jnp.sum(v, axis=0, keepdims=True) for v in sums], axis=0)

    expand(0, wide_a)

    def steps(first, count):
        for k in range(0, count, 2):
            expand(first + k + 1, wide_b)
            work(first + k, wide_a)
            expand(first + k + 2, wide_a)
            work(first + k + 1, wide_b)
        return 0

    long = total // UNROLL
    lax.fori_loop(0, long, lambda n, _: steps(n * UNROLL, UNROLL), 0)
    done = long * UNROLL
    lax.fori_loop(0, (total - done + 1) // 2, lambda n, _: steps(done + 2 * n, 2), 0)
    load_weights.wait()
    weight = weights_ref[...] * (4.0 / BLK * math.log(2.0) ** 2)
    grad_mon_ref[0 : UNITS * BLK, :] = grad_mon_ref[0 : UNITS * BLK, :] * column[...] * weight
    grad_out_ref[...] = grad_out_ref[...] * weight[None]


def scatter_kernel(
    mon_ref, flow_ref, grad_mon_ref, grad_out_ref,
    mon_in, y_in, y_sum, z_in, z_sum, last_in,
    gs, gr, fs, fr, zs, zr, ys, yr,
):
    o, p, e, z, c = position()
    own, group, same, along_z, across = peers(o, p, e, z, c)
    place = e * NX + o
    signals = enter(group, along_z, across)
    pl.semaphore_wait(pltpu.get_barrier_semaphore(), signals)

    order = (4, 3, 5, 2, 6, 1, 7, 0)
    crossed = {}
    for d in order:
        there = pl.ds(((1 - p) * NZ + low(z + d, NZ)) * SAME, SAME)
        crossed[d] = send(flow_ref.at[there], y_in.at[d], ys.at[d], yr.at[d], across)
    group_hops = []
    for d, (other, oo, oe, oc, device) in enumerate(group):
        rows = pl.ds(pl.multiple_of((oe * NC + oc) * MB * BLK + oo * OWN, 8), OWN)
        group_hops.append(send(mon_ref.at[rows], mon_in.at[d], gs.at[d], gr.at[d], device))
    hops = []
    for d in order:
        crossed[d].wait_recv()
        here = pl.ds((p * NZ + low(z + d, NZ)) * SAME, SAME)
        y_sum[d] = flow_ref[here] + y_in[d]
        if d > 0:
            hops.append(send(y_sum.at[d], z_in.at[d - 1], zs.at[d - 1], zr.at[d - 1], along_z[d][1]))
    for copy in crossed.values():
        copy.wait_send()
    for copy in hops:
        copy.wait()
    total = y_sum[0]
    for d in range(NZ - 1):
        total = total + z_in[d]
    z_sum[...] = total
    last_in[place] = z_sum[place]
    hops = [
        send(z_sum.at[other], last_in.at[place], fs.at[d], fr.at[d], device)
        for d, (other, device) in enumerate(same)
    ]
    for copy in group_hops:
        copy.wait()
    rows = pl.ds(pl.multiple_of((e * NC + c) * MB * BLK + o * OWN, 8), OWN)
    total = mon_ref[rows, :]
    for d in range(G - 1):
        total = total + mon_in[d]
    grad_mon_ref[...] = total
    for copy in hops:
        copy.wait()
    for m in range(SAME):
        grad_out_ref[m * KC : (m + 1) * KC, :] = last_in[m]


def store_kernel(mon_ref, flow_ref, mon_hbm, flow_hbm, sems):
    stores = [
        pltpu.make_async_copy(mon_ref, mon_hbm, sems.at[0]),
        pltpu.make_async_copy(flow_ref, flow_hbm, sems.at[1]),
    ]
    for store in stores:
        store.start()
    for store in stores:
        store.wait()


def vmem(count):
    return [pl.BlockSpec(memory_space=pltpu.VMEM)] * count


DMA = pltpu.SemaphoreType.DMA


def local(mon_flow, out_flow, rating, weights, lodf, tile_mon, tile_out, tile_count):
    inputs = [
        tile_mon[0], tile_out[0],
        lodf[0, 0], out_flow[0], rating.reshape(MB, BLK), mon_flow, weights.reshape(1, S),
    ]
    inputs = [pltpu.with_memory_space_constraint(x, pltpu.HBM) for x in inputs]
    tiles, gathered, mon_all, ratings, meta_all = pl.pallas_call(
        gather_kernel,
        out_shape=(
            jax.ShapeDtypeStruct((G, SLOTS * KC, BLK), BF16),
            jax.ShapeDtypeStruct((NP * NZ, SAME * KC, S), BF16),
            jax.ShapeDtypeStruct((2 * NC, MB * BLK, S), BF16),
            jax.ShapeDtypeStruct((2 * NC, MB, BLK), F32),
            jax.ShapeDtypeStruct((G, 1, S), jnp.int32),
        ),
        in_specs=[pl.BlockSpec(memory_space=pltpu.SMEM)] + [pl.BlockSpec(memory_space=pltpu.HBM)] * 6,
        out_specs=tuple(vmem(5)),
        scratch_shapes=[
            pltpu.SMEM((1, SLOTS), jnp.int32),
            pltpu.SMEM((1, SLOTS), jnp.int32),
            pltpu.VMEM((SLOTS, BLK, BLK), BF16),
            pltpu.VMEM((SAME * KC, S), BF16),
            pltpu.VMEM((G, SLOTS * KC, BLK), BF16),
            pltpu.VMEM((SAME, KC, S), F32),
            pltpu.VMEM((SAME, KC, S), F32),
            DMA((6,)), DMA((2, G - 1)), DMA((2, G - 1)), DMA((SAME - 1,)), DMA((SAME - 1,)),
            DMA((2, 2 * NC - 1)), DMA((2, 2 * NC - 1)), DMA((NZ - 1,)), DMA((NZ - 1,)), DMA((NZ,)), DMA((NZ,)),
        ],
        compiler_params=pltpu.CompilerParams(collective_id=0, has_side_effects=True, vmem_limit_bytes=VMEM_BYTES),
        name="gather",
    )(tile_count, *inputs[:6])

    part_mon, part_out = pl.pallas_call(
        tile_kernel,
        out_shape=(
            jax.ShapeDtypeStruct(((UNITS + 1) * BLK, S), F32),
            jax.ShapeDtypeStruct((SETS + 1, KC, S), F32),
        ),
        in_specs=vmem(5) + [pl.BlockSpec(memory_space=pltpu.HBM)],
        out_specs=tuple(vmem(2)),
        scratch_shapes=[
            pltpu.SMEM((G, 1, S), jnp.int32),
            pltpu.SMEM((G * SLOTS + 8,), jnp.int32),
            pltpu.SMEM((G * SLOTS + 8,), jnp.int32),
            pltpu.SMEM((G * SLOTS + 8,), jnp.int32),
            pltpu.VMEM((1, S), F32),
            DMA,
            DMA,
            pltpu.VMEM(((UNITS + 1) * BLK, S), F32),
            pltpu.VMEM((UNITS * BLK, S), F32),
            pltpu.VMEM((UNITS + 1, 1, BLK), F32),
            pltpu.VMEM((2 * KC, KC * S), BF16),
            pltpu.VMEM((G * SLOTS, KC, BLK), F32),
            pltpu.VMEM((SETS + 1, KC, S), F32),
            pltpu.VMEM((BLK, KC * S), F32),
            pltpu.VMEM((BLK, KC * S), F32),
        ],
        compiler_params=pltpu.CompilerParams(vmem_limit_bytes=VMEM_BYTES),
        name="tiles",
    )(meta_all, tiles, gathered, mon_all, ratings, inputs[6])

    grad_mon, grad_out = pl.pallas_call(
        scatter_kernel,
        out_shape=(
            jax.ShapeDtypeStruct((OWN, S), F32),
            jax.ShapeDtypeStruct((SAME * KC, S), F32),
        ),
        in_specs=vmem(2),
        out_specs=tuple(vmem(2)),
        scratch_shapes=[
            pltpu.VMEM((G - 1, OWN, S), F32),
            pltpu.VMEM((NZ, SAME, KC, S), F32),
            pltpu.VMEM((NZ, SAME, KC, S), F32),
            pltpu.VMEM((NZ - 1, SAME, KC, S), F32),
            pltpu.VMEM((SAME, KC, S), F32),
            pltpu.VMEM((SAME, KC, S), F32),
            DMA((G - 1,)), DMA((G - 1,)), DMA((SAME - 1,)), DMA((SAME - 1,)),
            DMA((NZ - 1,)), DMA((NZ - 1,)), DMA((NZ,)), DMA((NZ,)),
        ],
        compiler_params=pltpu.CompilerParams(
            collective_id=1, has_side_effects=True, vmem_limit_bytes=VMEM_BYTES
        ),
        name="scatter",
    )(part_mon, part_out)
    grad_mon, grad_out = pl.pallas_call(
        store_kernel,
        out_shape=(
            jax.ShapeDtypeStruct((OWN, S), F32),
            jax.ShapeDtypeStruct((SAME * KC, S), F32),
        ),
        in_specs=vmem(2),
        out_specs=tuple([pl.BlockSpec(memory_space=pltpu.HBM)] * 2),
        scratch_shapes=[DMA((2,))],
        compiler_params=pltpu.CompilerParams(vmem_limit_bytes=VMEM_BYTES),
        name="store",
    )(grad_mon, grad_out)
    return grad_mon, grad_out[None]


def solution(mesh):
    in_specs = (
        P("mon", None),
        P("out", "mon", None),
        P("mon"),
        P(),
        P("mon", "out", None, None, None),
        P("mon", "out", None),
        P("mon", "out", None),
        P("mon", "out"),
    )
    out_specs = (P(("mon", "out"), None), P("out", "mon", None))
    return jax.shard_map(local, mesh=mesh, in_specs=in_specs, out_specs=out_specs, check_vma=False)
```

```python
import functools
import math

import jax
import jax.numpy as jnp
from jax import lax
from jax.experimental import pallas as pl
from jax.experimental.pallas import tpu as pltpu
from jax.sharding import PartitionSpec as P

MESH = pl.DeviceIdType.MESH
NX, NY, NZ, NC = 4, 4, 8, 2
NP = NY // 2
SAME = 2 * NX
G = SAME * NC
BLK = 128
S = 128
SLOTS = 8
KC = BLK // G
MB = 3
UNROLL = 8
UNITS = 2 * NC * MB
SETS = NP * NZ * SAME
OWN = MB * BLK // NX
LOG2E = math.log2(math.e)
VMEM_BYTES = 16 << 20
F32 = jnp.float32
BF16 = jnp.bfloat16


def low(value, size):
    return value & (size - 1)


def high(value, size):
    return value >> (size.bit_length() - 1)


def position():
    i = lax.axis_index("mon")
    o = lax.axis_index("out")
    c = low(i, NC)
    z = low(high(i, NC), NZ)
    y = high(i, NC * NZ)
    p = high(y, 2)
    return o, p, low(y + p, 2), z, c


def at(o, p, e, z, c):
    y = 2 * p + low(e + p, 2)
    return ((y * NZ + z) * NC + c, o)


def peers(o, p, e, z, c):
    own = (c * 2 + e) * NX + o
    group = []
    for d in range(1, G):
        other = low(own + d, G)
        oo, oe, oc = low(other, NX), low(high(other, NX), 2), high(other, SAME)
        group.append((other, oo, oe, oc, at(oo, p, oe, z, oc)))
    same = []
    for d in range(1, SAME):
        other = low(e * NX + o + d, SAME)
        same.append((other, at(low(other, NX), p, high(other, NX), z, c)))
    along_z = {}
    for d in range(1, NZ):
        other = low(z + d, NZ)
        along_z[d] = (other, at(o, p, e, other, c))
    return own, group, same, along_z, at(o, 1 - p, e, z, c)


def enter(group, along_z, across):
    barrier = pltpu.get_barrier_semaphore()
    devices = [entry[-1] for entry in group] + [device for _, device in along_z.values()] + [across]
    for device in devices:
        pl.semaphore_signal(barrier, inc=1, device_id=device, device_id_type=MESH)
    return len(devices)


def send(src, dst, send_sem, recv_sem, device):
    copy = pltpu.make_async_remote_copy(
        src_ref=src, dst_ref=dst, send_sem=send_sem, recv_sem=recv_sem, device_id=device, device_id_type=MESH
    )
    copy.start()
    return copy


def gather_kernel(
    count_ref, tile_mon_hbm, tile_out_hbm, lodf_hbm, flow_hbm, rating_hbm, mon_hbm,
    tiles_ref, gathered_ref, mon_all_ref, rating_all_ref, meta_all_ref,
    tile_mon_ref, tile_out_ref, lodf_ref, flow_ref, tiles_out, flow_out, flow_in, loads, gs, gr, fs, fr, ms, mr, zs, zr, ys, yr,
):
    o, p, e, z, c = position()
    place = e * NX + o
    unit = e * NC + c
    load_flow = pltpu.make_async_copy(flow_hbm, flow_ref, loads.at[0])
    load_lodf = pltpu.make_async_copy(lodf_hbm, lodf_ref, loads.at[1])
    load_mon = pltpu.make_async_copy(mon_hbm, mon_all_ref.at[unit], loads.at[2])
    load_rating = pltpu.make_async_copy(rating_hbm, rating_all_ref.at[unit], loads.at[3])
    words_in = [
        pltpu.make_async_copy(tile_mon_hbm, tile_mon_ref, loads.at[4]),
        pltpu.make_async_copy(tile_out_hbm, tile_out_ref, loads.at[5]),
    ]
    for load in [load_flow, load_lodf, load_mon, load_rating] + words_in:
        load.start()
    own, group, same, along_z, across = peers(o, p, e, z, c)
    signals = enter(group, along_z, across)
    for load in words_in:
        load.wait()
    lane = lax.broadcasted_iota(jnp.int32, (1, S), 1)
    words = jnp.where(lane == 2 * SLOTS, count_ref[0, 0], 0)
    for q in range(SLOTS):
        block = tile_out_ref[0, q]
        across_y = block // NZ
        pair = across_y // 2
        row = (pair * NZ + lax.rem(block, NZ)) * SAME + lax.rem(across_y + pair, 2) * NX + o
        words = jnp.where(lane == q, unit * MB + tile_mon_ref[0, q], words)
        words = jnp.where(lane == SLOTS + q, row, words)
    meta_all_ref[own] = words
    load_flow.wait()
    flow_out[...] = flow_ref[...].astype(F32).reshape(SAME, KC, S)
    flow_in[place] = flow_out[place]
    load_lodf.wait()
    for q in range(0, SLOTS, 2):
        first = jnp.transpose(lodf_ref[q].astype(F32))
        second = jnp.transpose(lodf_ref[q + 1].astype(F32))
        for m in range(G):
            rows = slice(m * KC, (m + 1) * KC)
            tiles_out[m, q * KC : (q + 2) * KC, :] = jnp.concatenate([first[rows], second[rows]], axis=0).astype(BF16)
    tiles_ref[own] = tiles_out[own]
    load_mon.wait()
    load_rating.wait()

    pl.semaphore_wait(pltpu.get_barrier_semaphore(), signals)
    flows = [
        send(flow_out.at[other], flow_in.at[place], fs.at[d], fr.at[d], device)
        for d, (other, device) in enumerate(same)
    ]
    rest = []
    for d, (other, _, _, _, device) in enumerate(group):
        rest.append(send(tiles_out.at[other], tiles_ref.at[own], gs.at[0, d], gr.at[0, d], device))
    for d, (other, _, _, _, device) in enumerate(group):
        rest.append(send(meta_all_ref.at[own], meta_all_ref.at[own], gs.at[1, d], gr.at[1, d], device))
    for d in range(1, 2 * NC):
        other = low(unit + d, 2 * NC)
        device = at(o, p, high(other, NC), z, low(other, NC))
        rest.append(send(mon_all_ref.at[unit], mon_all_ref.at[unit], ms.at[0, d - 1], mr.at[0, d - 1], device))
        rest.append(send(rating_all_ref.at[unit], rating_all_ref.at[unit], ms.at[1, d - 1], mr.at[1, d - 1], device))
    for copy in flows:
        copy.wait()
    mine = p * NZ + z
    gathered_ref[mine] = flow_in[...].reshape(SAME * KC, S).astype(BF16)
    block = gathered_ref.at[mine]
    hops = {}
    for d in (4, 3, 5, 2, 6, 1, 7):
        hops[d] = send(block, block, zs.at[d - 1], zr.at[d - 1], along_z[d][1])
    crossed = [send(block, block, ys.at[0], yr.at[0], across)]
    for d in (1, 7, 2, 6, 3, 5, 4):
        hops[d].wait_recv()
        block = gathered_ref.at[p * NZ + low(z + NZ - d, NZ)]
        crossed.append(send(block, block, ys.at[d], yr.at[d], across))
    for copy in hops.values():
        copy.wait_send()
    for copy in rest + crossed:
        copy.wait()


def tile_kernel(
    words_ref, tiles_ref, flow_ref, mon_ref, rating_ref, weights_hbm,
    grad_mon_ref, grad_out_ref,
    meta_ref, from_list, block_list, set_list, weights_ref, load, load_words, scaled, column, row_scale, spread, pieces, flows, wide_a, wide_b,
):
    load_weights = pltpu.make_async_copy(weights_hbm, weights_ref, load)
    load_weights.start()
    words = pltpu.make_async_copy(words_ref, meta_ref, load_words)
    words.start()
    for u in range(2 * NC):
        for t in range(MB):
            b = u * MB + t
            scale = math.sqrt(LOG2E) / rating_ref[u, t : t + 1, :]
            row_scale[b, :, :] = scale
            turned = jnp.transpose(jnp.broadcast_to(scale, (BLK, BLK)))
            column[b * BLK : (b + 1) * BLK, :] = turned
            scaled[b * BLK : (b + 1) * BLK, :] = turned * mon_ref[u, t * BLK : (t + 1) * BLK, :].astype(F32)
    row_scale[UNITS, :, :] = jnp.zeros((1, BLK), F32)
    scaled[UNITS * BLK :, :] = jnp.zeros((BLK, S), F32)
    grad_mon_ref[...] = jnp.zeros_like(grad_mon_ref)
    grad_out_ref[...] = jnp.zeros_like(grad_out_ref)
    pieces[...] = tiles_ref[...].astype(F32).reshape(G * SLOTS, KC, BLK)
    flows[0:SETS] = flow_ref[...].astype(F32).reshape(SETS, KC, S)
    flows[SETS] = jnp.zeros((KC, S), F32)
    term = lax.broadcasted_iota(jnp.int32, spread.shape, 0)
    lane = lax.broadcasted_iota(jnp.int32, spread.shape, 1)
    spread[...] = jnp.where(lax.rem(term, KC) == lane // S, 1.0, 0.0).astype(BF16)

    words.wait()

    def list_member(member, total):
        count = meta_ref[member, 0, 2 * SLOTS]

        def add(q, _):
            from_list[total + q] = member * SLOTS + q
            block_list[total + q] = meta_ref[member, 0, q]
            set_list[total + q] = meta_ref[member, 0, SLOTS + q]
            return 0

        lax.fori_loop(0, count, add, 0)
        return total + count

    total = lax.fori_loop(0, G, list_member, 0)
    for extra in range(3):
        from_list[total + extra] = 0
        block_list[total + extra] = UNITS
        set_list[total + extra] = SETS

    def expand(n, wide):
        piece = pieces[from_list[n]] * row_scale[block_list[n]]
        high = piece.astype(BF16).astype(F32)
        both = jnp.concatenate([high, piece - high], axis=0).astype(BF16)
        wide[...] = lax.dot_general(both, spread[...], (((0,), (0,)), ((), ())), preferred_element_type=F32)

    def work(n, wide):
        row = set_list[n]
        start = pl.multiple_of(block_list[n] * BLK, BLK)
        flow = [flows[row, pl.ds(j, 8, stride=0), :] for j in range(KC)]
        sums = [None] * KC
        for i in range(BLK // 8):
            base = scaled[pl.ds(start + i * 8, 8), :]
            total_m = None
            for j in range(KC):
                factor = wide[i * 8 : (i + 1) * 8, j * S : (j + 1) * S]
                post = base + factor * flow[j]
                square = post * post
                level = jnp.log2(jnp.exp2(square) + math.e)
                slope = (level - LOG2E) * jnp.exp2(square - level) * post
                total_m = slope if total_m is None else total_m + slope
                part = factor * slope
                sums[j] = part if sums[j] is None else sums[j] + part
            grad_mon_ref[pl.ds(start + i * 8, 8), :] += total_m
        grad_out_ref[row] += jnp.concatenate([jnp.sum(v, axis=0, keepdims=True) for v in sums], axis=0)

    expand(0, wide_a)

    def steps(first, count):
        for k in range(0, count, 2):
            expand(first + k + 1, wide_b)
            work(first + k, wide_a)
            expand(first + k + 2, wide_a)
            work(first + k + 1, wide_b)
        return 0

    long = total // UNROLL
    lax.fori_loop(0, long, lambda n, _: steps(n * UNROLL, UNROLL), 0)
    done = long * UNROLL
    lax.fori_loop(0, (total - done + 1) // 2, lambda n, _: steps(done + 2 * n, 2), 0)
    load_weights.wait()
    weight = weights_ref[...] * (4.0 / BLK * math.log(2.0) ** 2)
    grad_mon_ref[0 : UNITS * BLK, :] = grad_mon_ref[0 : UNITS * BLK, :] * column[...] * weight
    grad_out_ref[...] = grad_out_ref[...] * weight[None]


def scatter_kernel(
    mon_ref, flow_ref, grad_mon_ref, grad_out_ref,
    mon_in, y_in, y_sum, z_in, z_sum, last_in,
    gs, gr, fs, fr, zs, zr, ys, yr,
):
    o, p, e, z, c = position()
    own, group, same, along_z, across = peers(o, p, e, z, c)
    place = e * NX + o
    signals = enter(group, along_z, across)
    pl.semaphore_wait(pltpu.get_barrier_semaphore(), signals)

    order = (4, 3, 5, 2, 6, 1, 7, 0)
    crossed = {}
    for d in order:
        there = pl.ds(((1 - p) * NZ + low(z + d, NZ)) * SAME, SAME)
        crossed[d] = send(flow_ref.at[there], y_in.at[d], ys.at[d], yr.at[d], across)
    for d, (other, oo, oe, oc, device) in enumerate(group):
        rows = pl.ds(pl.multiple_of((oe * NC + oc) * MB * BLK + oo * OWN, 8), OWN)
        send(mon_ref.at[rows], mon_in.at[d], gs, gr, device)
    hops = []
    for d in order:
        crossed[d].wait_recv()
        here = pl.ds((p * NZ + low(z + d, NZ)) * SAME, SAME)
        y_sum[d] = flow_ref[here] + y_in[d]
        if d > 0:
            hops.append(send(y_sum.at[d], z_in.at[d - 1], zs.at[d - 1], zr.at[d - 1], along_z[d][1]))
    for copy in crossed.values():
        copy.wait_send()
    for copy in hops:
        copy.wait()
    total = y_sum[0]
    for d in range(NZ - 1):
        total = total + z_in[d]
    z_sum[...] = total
    last_in[place] = z_sum[place]
    hops = [
        send(z_sum.at[other], last_in.at[place], fs.at[d], fr.at[d], device)
        for d, (other, device) in enumerate(same)
    ]
    for sem in (gs, gr):
        pltpu.make_async_copy(mon_in, mon_in, sem).wait()
    rows = pl.ds(pl.multiple_of((e * NC + c) * MB * BLK + o * OWN, 8), OWN)
    total = mon_ref[rows, :]
    for d in range(G - 1):
        total = total + mon_in[d]
    grad_mon_ref[...] = total
    for copy in hops:
        copy.wait()
    for m in range(SAME):
        grad_out_ref[m * KC : (m + 1) * KC, :] = last_in[m]


def store_kernel(mon_ref, flow_ref, mon_hbm, flow_hbm, sems):
    stores = [
        pltpu.make_async_copy(mon_ref, mon_hbm, sems.at[0]),
        pltpu.make_async_copy(flow_ref, flow_hbm, sems.at[1]),
    ]
    for store in stores:
        store.start()
    for store in stores:
        store.wait()


def vmem(count):
    return [pl.BlockSpec(memory_space=pltpu.VMEM)] * count


DMA = pltpu.SemaphoreType.DMA


def local(mon_flow, out_flow, rating, weights, lodf, tile_mon, tile_out, tile_count):
    inputs = [
        tile_mon[0], tile_out[0],
        lodf[0, 0], out_flow[0], rating.reshape(MB, BLK), mon_flow, weights.reshape(1, S),
    ]
    inputs = [pltpu.with_memory_space_constraint(x, pltpu.HBM) for x in inputs]
    tiles, gathered, mon_all, ratings, meta_all = pl.pallas_call(
        gather_kernel,
        out_shape=(
            jax.ShapeDtypeStruct((G, SLOTS * KC, BLK), BF16),
            jax.ShapeDtypeStruct((NP * NZ, SAME * KC, S), BF16),
            jax.ShapeDtypeStruct((2 * NC, MB * BLK, S), BF16),
            jax.ShapeDtypeStruct((2 * NC, MB, BLK), F32),
            jax.ShapeDtypeStruct((G, 1, S), jnp.int32),
        ),
        in_specs=[pl.BlockSpec(memory_space=pltpu.SMEM)] + [pl.BlockSpec(memory_space=pltpu.HBM)] * 6,
        out_specs=tuple(vmem(5)),
        scratch_shapes=[
            pltpu.SMEM((1, SLOTS), jnp.int32),
            pltpu.SMEM((1, SLOTS), jnp.int32),
            pltpu.VMEM((SLOTS, BLK, BLK), BF16),
            pltpu.VMEM((SAME * KC, S), BF16),
            pltpu.VMEM((G, SLOTS * KC, BLK), BF16),
            pltpu.VMEM((SAME, KC, S), F32),
            pltpu.VMEM((SAME, KC, S), F32),
            DMA((6,)), DMA((2, G - 1)), DMA((2, G - 1)), DMA((SAME - 1,)), DMA((SAME - 1,)),
            DMA((2, 2 * NC - 1)), DMA((2, 2 * NC - 1)), DMA((NZ - 1,)), DMA((NZ - 1,)), DMA((NZ,)), DMA((NZ,)),
        ],
        compiler_params=pltpu.CompilerParams(collective_id=0, has_side_effects=True, vmem_limit_bytes=VMEM_BYTES),
        name="gather",
    )(tile_count, *inputs[:6])

    part_mon, part_out = pl.pallas_call(
        tile_kernel,
        out_shape=(
            jax.ShapeDtypeStruct(((UNITS + 1) * BLK, S), F32),
            jax.ShapeDtypeStruct((SETS + 1, KC, S), F32),
        ),
        in_specs=vmem(5) + [pl.BlockSpec(memory_space=pltpu.HBM)],
        out_specs=tuple(vmem(2)),
        scratch_shapes=[
            pltpu.SMEM((G, 1, S), jnp.int32),
            pltpu.SMEM((G * SLOTS + 8,), jnp.int32),
            pltpu.SMEM((G * SLOTS + 8,), jnp.int32),
            pltpu.SMEM((G * SLOTS + 8,), jnp.int32),
            pltpu.VMEM((1, S), F32),
            DMA,
            DMA,
            pltpu.VMEM(((UNITS + 1) * BLK, S), F32),
            pltpu.VMEM((UNITS * BLK, S), F32),
            pltpu.VMEM((UNITS + 1, 1, BLK), F32),
            pltpu.VMEM((2 * KC, KC * S), BF16),
            pltpu.VMEM((G * SLOTS, KC, BLK), F32),
            pltpu.VMEM((SETS + 1, KC, S), F32),
            pltpu.VMEM((BLK, KC * S), F32),
            pltpu.VMEM((BLK, KC * S), F32),
        ],
        compiler_params=pltpu.CompilerParams(vmem_limit_bytes=VMEM_BYTES),
        name="tiles",
    )(meta_all, tiles, gathered, mon_all, ratings, inputs[6])

    grad_mon, grad_out = pl.pallas_call(
        scatter_kernel,
        out_shape=(
            jax.ShapeDtypeStruct((OWN, S), F32),
            jax.ShapeDtypeStruct((SAME * KC, S), F32),
        ),
        in_specs=vmem(2),
        out_specs=tuple(vmem(2)),
        scratch_shapes=[
            pltpu.VMEM((G - 1, OWN, S), F32),
            pltpu.VMEM((NZ, SAME, KC, S), F32),
            pltpu.VMEM((NZ, SAME, KC, S), F32),
            pltpu.VMEM((NZ - 1, SAME, KC, S), F32),
            pltpu.VMEM((SAME, KC, S), F32),
            pltpu.VMEM((SAME, KC, S), F32),
            DMA, DMA, DMA((SAME - 1,)), DMA((SAME - 1,)),
            DMA((NZ - 1,)), DMA((NZ - 1,)), DMA((NZ,)), DMA((NZ,)),
        ],
        compiler_params=pltpu.CompilerParams(
            collective_id=1, has_side_effects=True, vmem_limit_bytes=VMEM_BYTES
        ),
        name="scatter",
    )(part_mon, part_out)
    grad_mon, grad_out = pl.pallas_call(
        store_kernel,
        out_shape=(
            jax.ShapeDtypeStruct((OWN, S), F32),
            jax.ShapeDtypeStruct((SAME * KC, S), F32),
        ),
        in_specs=vmem(2),
        out_specs=tuple([pl.BlockSpec(memory_space=pltpu.HBM)] * 2),
        scratch_shapes=[DMA((2,))],
        compiler_params=pltpu.CompilerParams(vmem_limit_bytes=VMEM_BYTES),
        name="store",
    )(grad_mon, grad_out)
    return grad_mon, grad_out[None]


def solution(mesh):
    in_specs = (
        P("mon", None),
        P("out", "mon", None),
        P("mon"),
        P(),
        P("mon", "out", None, None, None),
        P("mon", "out", None),
        P("mon", "out", None),
        P("mon", "out"),
    )
    out_specs = (P(("mon", "out"), None), P("out", "mon", None))
    return jax.shard_map(local, mesh=mesh, in_specs=in_specs, out_specs=out_specs, check_vma=False)
```

```python
import functools
import math

import jax
import jax.numpy as jnp
from jax import lax
from jax.experimental import pallas as pl
from jax.experimental.pallas import tpu as pltpu
from jax.sharding import PartitionSpec as P

MESH = pl.DeviceIdType.MESH
NX, NY, NZ, NC = 4, 4, 8, 2
NP = NY // 2
SAME = 2 * NX
G = SAME * NC
BLK = 128
S = 128
SLOTS = 8
KC = BLK // G
MB = 3
UNROLL = 8
UNITS = 2 * NC * MB
SETS = NP * NZ * SAME
OWN = MB * BLK // NX
LOG2E = math.log2(math.e)
VMEM_BYTES = 16 << 20
F32 = jnp.float32
BF16 = jnp.bfloat16


def low(value, size):
    return value & (size - 1)


def high(value, size):
    return value >> (size.bit_length() - 1)


def position():
    i = lax.axis_index("mon")
    o = lax.axis_index("out")
    c = low(i, NC)
    z = low(high(i, NC), NZ)
    y = high(i, NC * NZ)
    p = high(y, 2)
    return o, p, low(y + p, 2), z, c


def at(o, p, e, z, c):
    y = 2 * p + low(e + p, 2)
    return ((y * NZ + z) * NC + c, o)


def peers(o, p, e, z, c):
    own = (c * 2 + e) * NX + o
    group = []
    for d in range(1, G):
        other = low(own + d, G)
        oo, oe, oc = low(other, NX), low(high(other, NX), 2), high(other, SAME)
        group.append((other, oo, oe, oc, at(oo, p, oe, z, oc)))
    same = []
    for d in range(1, SAME):
        other = low(e * NX + o + d, SAME)
        same.append((other, at(low(other, NX), p, high(other, NX), z, c)))
    along_z = {}
    for d in range(1, NZ):
        other = low(z + d, NZ)
        along_z[d] = (other, at(o, p, e, other, c))
    return own, group, same, along_z, at(o, 1 - p, e, z, c)


def enter(group, along_z, across):
    barrier = pltpu.get_barrier_semaphore()
    devices = [entry[-1] for entry in group] + [device for _, device in along_z.values()] + [across]
    for device in devices:
        pl.semaphore_signal(barrier, inc=1, device_id=device, device_id_type=MESH)
    return len(devices)


def send(src, dst, send_sem, recv_sem, device):
    copy = pltpu.make_async_remote_copy(
        src_ref=src, dst_ref=dst, send_sem=send_sem, recv_sem=recv_sem, device_id=device, device_id_type=MESH
    )
    copy.start()
    return copy


def gather_kernel(
    count_ref, tile_mon_hbm, tile_out_hbm, lodf_hbm, flow_hbm, rating_hbm, mon_hbm,
    tiles_ref, gathered_ref, mon_all_ref, rating_all_ref, meta_all_ref,
    tile_mon_ref, tile_out_ref, lodf_ref, flow_ref, tiles_out, flow_out, flow_in, loads, gs, gr, fs, fr, ms, mr, zs, zr, ys, yr,
):
    o, p, e, z, c = position()
    place = e * NX + o
    unit = e * NC + c
    load_flow = pltpu.make_async_copy(flow_hbm, flow_ref, loads.at[0])
    load_lodf = pltpu.make_async_copy(lodf_hbm, lodf_ref, loads.at[1])
    load_mon = pltpu.make_async_copy(mon_hbm, mon_all_ref.at[unit], loads.at[2])
    load_rating = pltpu.make_async_copy(rating_hbm, rating_all_ref.at[unit], loads.at[3])
    words_in = [
        pltpu.make_async_copy(tile_mon_hbm, tile_mon_ref, loads.at[4]),
        pltpu.make_async_copy(tile_out_hbm, tile_out_ref, loads.at[5]),
    ]
    for load in [load_flow, load_lodf, load_mon, load_rating] + words_in:
        load.start()
    own, group, same, along_z, across = peers(o, p, e, z, c)
    signals = enter(group, along_z, across)
    for load in words_in:
        load.wait()
    lane = lax.broadcasted_iota(jnp.int32, (1, S), 1)
    words = jnp.where(lane == 2 * SLOTS, count_ref[0, 0], 0)
    for q in range(SLOTS):
        block = tile_out_ref[0, q]
        across_y = block // NZ
        pair = across_y // 2
        row = (pair * NZ + lax.rem(block, NZ)) * SAME + lax.rem(across_y + pair, 2) * NX + o
        words = jnp.where(lane == q, unit * MB + tile_mon_ref[0, q], words)
        words = jnp.where(lane == SLOTS + q, row, words)
    meta_all_ref[own] = words
    load_flow.wait()
    flow_out[...] = flow_ref[...].astype(F32).reshape(SAME, KC, S)
    flow_in[place] = flow_out[place]
    load_lodf.wait()
    for q in range(0, SLOTS, 2):
        first = jnp.transpose(lodf_ref[q].astype(F32))
        second = jnp.transpose(lodf_ref[q + 1].astype(F32))
        for m in range(G):
            rows = slice(m * KC, (m + 1) * KC)
            tiles_out[m, q * KC : (q + 2) * KC, :] = jnp.concatenate([first[rows], second[rows]], axis=0).astype(BF16)
    tiles_ref[own] = tiles_out[own]
    load_mon.wait()
    load_rating.wait()

    pl.semaphore_wait(pltpu.get_barrier_semaphore(), signals)
    flows = [
        send(flow_out.at[other], flow_in.at[place], fs.at[d], fr.at[d], device)
        for d, (other, device) in enumerate(same)
    ]
    rest = []
    for d, (other, _, _, _, device) in enumerate(group):
        rest.append(send(tiles_out.at[other], tiles_ref.at[own], gs.at[0, d], gr.at[0, d], device))
    for d, (other, _, _, _, device) in enumerate(group):
        rest.append(send(meta_all_ref.at[own], meta_all_ref.at[own], gs.at[1, d], gr.at[1, d], device))
    for d in range(1, 2 * NC):
        other = low(unit + d, 2 * NC)
        device = at(o, p, high(other, NC), z, low(other, NC))
        rest.append(send(mon_all_ref.at[unit], mon_all_ref.at[unit], ms.at[0, d - 1], mr.at[0, d - 1], device))
        rest.append(send(rating_all_ref.at[unit], rating_all_ref.at[unit], ms.at[1, d - 1], mr.at[1, d - 1], device))
    for copy in flows:
        copy.wait()
    mine = p * NZ + z
    gathered_ref[mine] = flow_in[...].reshape(SAME * KC, S).astype(BF16)
    block = gathered_ref.at[mine]
    hops = {}
    for d in (4, 3, 5, 2, 6, 1, 7):
        hops[d] = send(block, block, zs.at[d - 1], zr.at[d - 1], along_z[d][1])
    crossed = [send(block, block, ys.at[0], yr.at[0], across)]
    for d in (1, 7, 2, 6, 3, 5, 4):
        hops[d].wait_recv()
        block = gathered_ref.at[p * NZ + low(z + NZ - d, NZ)]
        crossed.append(send(block, block, ys.at[d], yr.at[d], across))
    for copy in hops.values():
        copy.wait_send()
    for copy in rest + crossed:
        copy.wait()


def tile_kernel(
    words_ref, tiles_ref, flow_ref, mon_ref, rating_ref, weights_hbm,
    grad_mon_ref, grad_out_ref,
    meta_ref, from_list, block_list, set_list, weights_ref, load, load_words, scaled, column, row_scale, spread, pieces, flows, wide_a, wide_b,
):
    load_weights = pltpu.make_async_copy(weights_hbm, weights_ref, load)
    load_weights.start()
    words = pltpu.make_async_copy(words_ref, meta_ref, load_words)
    words.start()
    for u in range(2 * NC):
        for t in range(MB):
            b = u * MB + t
            scale = math.sqrt(LOG2E) / rating_ref[u, t : t + 1, :]
            row_scale[b, :, :] = scale
            turned = jnp.transpose(jnp.broadcast_to(scale, (BLK, BLK)))
            column[b * BLK : (b + 1) * BLK, :] = turned
            scaled[b * BLK : (b + 1) * BLK, :] = turned * mon_ref[u, t * BLK : (t + 1) * BLK, :].astype(F32)
    row_scale[UNITS, :, :] = jnp.zeros((1, BLK), F32)
    scaled[UNITS * BLK :, :] = jnp.zeros((BLK, S), F32)
    grad_mon_ref[...] = jnp.zeros_like(grad_mon_ref)
    grad_out_ref[...] = jnp.zeros_like(grad_out_ref)
    pieces[...] = tiles_ref[...].astype(F32).reshape(G * SLOTS, KC, BLK)
    flows[0:SETS] = flow_ref[...].astype(F32).reshape(SETS, KC, S)
    flows[SETS] = jnp.zeros((KC, S), F32)
    term = lax.broadcasted_iota(jnp.int32, spread.shape, 0)
    lane = lax.broadcasted_iota(jnp.int32, spread.shape, 1)
    spread[...] = jnp.where(lax.rem(term, KC) == lane // S, 1.0, 0.0).astype(BF16)

    words.wait()

    def list_member(member, total):
        count = meta_ref[member, 0, 2 * SLOTS]

        def add(q, _):
            from_list[total + q] = member * SLOTS + q
            block_list[total + q] = meta_ref[member, 0, q]
            set_list[total + q] = meta_ref[member, 0, SLOTS + q]
            return 0

        lax.fori_loop(0, count, add, 0)
        return total + count

    total = lax.fori_loop(0, G, list_member, 0)
    for extra in range(3):
        from_list[total + extra] = 0
        block_list[total + extra] = UNITS
        set_list[total + extra] = SETS

    def expand(n, wide):
        piece = pieces[from_list[n]] * row_scale[block_list[n]]
        high = piece.astype(BF16).astype(F32)
        both = jnp.concatenate([high, piece - high], axis=0).astype(BF16)
        wide[...] = lax.dot_general(both, spread[...], (((0,), (0,)), ((), ())), preferred_element_type=F32)

    def work(n, wide):
        row = set_list[n]
        start = pl.multiple_of(block_list[n] * BLK, BLK)
        flow = [flows[row, pl.ds(j, 8, stride=0), :] for j in range(KC)]
        sums = [None] * KC
        for i in range(BLK // 8):
            base = scaled[pl.ds(start + i * 8, 8), :]
            total_m = None
            for j in range(KC):
                factor = wide[i * 8 : (i + 1) * 8, j * S : (j + 1) * S]
                post = base + factor * flow[j]
                square = post * post
                level = jnp.log2(jnp.exp2(square) + math.e)
                slope = (level - LOG2E) * jnp.exp2(square - level) * post
                total_m = slope if total_m is None else total_m + slope
                part = factor * slope
                sums[j] = part if sums[j] is None else sums[j] + part
            grad_mon_ref[pl.ds(start + i * 8, 8), :] += total_m
        grad_out_ref[row] += jnp.concatenate([jnp.sum(v, axis=0, keepdims=True) for v in sums], axis=0)

    expand(0, wide_a)

    def steps(first, count):
        for k in range(0, count, 2):
            expand(first + k + 1, wide_b)
            work(first + k, wide_a)
            expand(first + k + 2, wide_a)
            work(first + k + 1, wide_b)
        return 0

    long = total // UNROLL
    lax.fori_loop(0, long, lambda n, _: steps(n * UNROLL, UNROLL), 0)
    done = long * UNROLL
    lax.fori_loop(0, (total - done + 1) // 2, lambda n, _: steps(done + 2 * n, 2), 0)
    load_weights.wait()
    weight = weights_ref[...] * (4.0 / BLK * math.log(2.0) ** 2)
    grad_mon_ref[0 : UNITS * BLK, :] = grad_mon_ref[0 : UNITS * BLK, :] * column[...] * weight
    grad_out_ref[...] = grad_out_ref[...] * weight[None]


def scatter_kernel(
    mon_ref, flow_ref, grad_mon_ref, grad_out_ref,
    mon_in, y_in, y_sum, z_in, z_sum, last_in,
    gs, gr, fs, fr, zs, zr, ys, yr,
):
    o, p, e, z, c = position()
    own, group, same, along_z, across = peers(o, p, e, z, c)
    place = e * NX + o
    signals = enter(group, along_z, across)
    pl.semaphore_wait(pltpu.get_barrier_semaphore(), signals)

    order = (4, 3, 5, 2, 6, 1, 7, 0)
    crossed = {}
    for d in order:
        there = pl.ds(((1 - p) * NZ + low(z + d, NZ)) * SAME, SAME)
        crossed[d] = send(flow_ref.at[there], y_in.at[d], ys.at[d], yr.at[d], across)
    for d, (other, oo, oe, oc, device) in enumerate(group):
        rows = pl.ds(pl.multiple_of((oe * NC + oc) * MB * BLK + oo * OWN, 8), OWN)
        send(mon_ref.at[rows], mon_in.at[d], gs, gr, device)
    hops = []
    for d in order:
        crossed[d].wait_recv()
        here = pl.ds((p * NZ + low(z + d, NZ)) * SAME, SAME)
        y_sum[d] = flow_ref[here] + y_in[d]
        if d > 0:
            hops.append(send(y_sum.at[d], z_in.at[d - 1], zs.at[d - 1], zr.at[d - 1], along_z[d][1]))
    for copy in crossed.values():
        copy.wait_send()
    for copy in hops:
        copy.wait()
    total = y_sum[0]
    for d in range(NZ - 1):
        total = total + z_in[d]
    z_sum[...] = total
    last_in[place] = z_sum[place]
    hops = [
        send(z_sum.at[other], last_in.at[place], fs, fr, device)
        for d, (other, device) in enumerate(same)
    ]
    for sem in (gs, gr):
        pltpu.make_async_copy(mon_in, mon_in, sem).wait()
    rows = pl.ds(pl.multiple_of((e * NC + c) * MB * BLK + o * OWN, 8), OWN)
    total = mon_ref[rows, :]
    for d in range(G - 1):
        total = total + mon_in[d]
    grad_mon_ref[...] = total
    most = last_in.at[pl.ds(0, SAME - 1)]
    for sem in (fs, fr):
        pltpu.make_async_copy(most, most, sem).wait()
    for m in range(SAME):
        grad_out_ref[m * KC : (m + 1) * KC, :] = last_in[m]


def store_kernel(mon_ref, flow_ref, mon_hbm, flow_hbm, sems):
    stores = [
        pltpu.make_async_copy(mon_ref, mon_hbm, sems.at[0]),
        pltpu.make_async_copy(flow_ref, flow_hbm, sems.at[1]),
    ]
    for store in stores:
        store.start()
    for store in stores:
        store.wait()


def vmem(count):
    return [pl.BlockSpec(memory_space=pltpu.VMEM)] * count


DMA = pltpu.SemaphoreType.DMA


def local(mon_flow, out_flow, rating, weights, lodf, tile_mon, tile_out, tile_count):
    inputs = [
        tile_mon[0], tile_out[0],
        lodf[0, 0], out_flow[0], rating.reshape(MB, BLK), mon_flow, weights.reshape(1, S),
    ]
    inputs = [pltpu.with_memory_space_constraint(x, pltpu.HBM) for x in inputs]
    tiles, gathered, mon_all, ratings, meta_all = pl.pallas_call(
        gather_kernel,
        out_shape=(
            jax.ShapeDtypeStruct((G, SLOTS * KC, BLK), BF16),
            jax.ShapeDtypeStruct((NP * NZ, SAME * KC, S), BF16),
            jax.ShapeDtypeStruct((2 * NC, MB * BLK, S), BF16),
            jax.ShapeDtypeStruct((2 * NC, MB, BLK), F32),
            jax.ShapeDtypeStruct((G, 1, S), jnp.int32),
        ),
        in_specs=[pl.BlockSpec(memory_space=pltpu.SMEM)] + [pl.BlockSpec(memory_space=pltpu.HBM)] * 6,
        out_specs=tuple(vmem(5)),
        scratch_shapes=[
            pltpu.SMEM((1, SLOTS), jnp.int32),
            pltpu.SMEM((1, SLOTS), jnp.int32),
            pltpu.VMEM((SLOTS, BLK, BLK), BF16),
            pltpu.VMEM((SAME * KC, S), BF16),
            pltpu.VMEM((G, SLOTS * KC, BLK), BF16),
            pltpu.VMEM((SAME, KC, S), F32),
            pltpu.VMEM((SAME, KC, S), F32),
            DMA((6,)), DMA((2, G - 1)), DMA((2, G - 1)), DMA((SAME - 1,)), DMA((SAME - 1,)),
            DMA((2, 2 * NC - 1)), DMA((2, 2 * NC - 1)), DMA((NZ - 1,)), DMA((NZ - 1,)), DMA((NZ,)), DMA((NZ,)),
        ],
        compiler_params=pltpu.CompilerParams(collective_id=0, has_side_effects=True, vmem_limit_bytes=VMEM_BYTES),
        name="gather",
    )(tile_count, *inputs[:6])

    part_mon, part_out = pl.pallas_call(
        tile_kernel,
        out_shape=(
            jax.ShapeDtypeStruct(((UNITS + 1) * BLK, S), F32),
            jax.ShapeDtypeStruct((SETS + 1, KC, S), F32),
        ),
        in_specs=vmem(5) + [pl.BlockSpec(memory_space=pltpu.HBM)],
        out_specs=tuple(vmem(2)),
        scratch_shapes=[
            pltpu.SMEM((G, 1, S), jnp.int32),
            pltpu.SMEM((G * SLOTS + 8,), jnp.int32),
            pltpu.SMEM((G * SLOTS + 8,), jnp.int32),
            pltpu.SMEM((G * SLOTS + 8,), jnp.int32),
            pltpu.VMEM((1, S), F32),
            DMA,
            DMA,
            pltpu.VMEM(((UNITS + 1) * BLK, S), F32),
            pltpu.VMEM((UNITS * BLK, S), F32),
            pltpu.VMEM((UNITS + 1, 1, BLK), F32),
            pltpu.VMEM((2 * KC, KC * S), BF16),
            pltpu.VMEM((G * SLOTS, KC, BLK), F32),
            pltpu.VMEM((SETS + 1, KC, S), F32),
            pltpu.VMEM((BLK, KC * S), F32),
            pltpu.VMEM((BLK, KC * S), F32),
        ],
        compiler_params=pltpu.CompilerParams(vmem_limit_bytes=VMEM_BYTES),
        name="tiles",
    )(meta_all, tiles, gathered, mon_all, ratings, inputs[6])

    grad_mon, grad_out = pl.pallas_call(
        scatter_kernel,
        out_shape=(
            jax.ShapeDtypeStruct((OWN, S), F32),
            jax.ShapeDtypeStruct((SAME * KC, S), F32),
        ),
        in_specs=vmem(2),
        out_specs=tuple(vmem(2)),
        scratch_shapes=[
            pltpu.VMEM((G - 1, OWN, S), F32),
            pltpu.VMEM((NZ, SAME, KC, S), F32),
            pltpu.VMEM((NZ, SAME, KC, S), F32),
            pltpu.VMEM((NZ - 1, SAME, KC, S), F32),
            pltpu.VMEM((SAME, KC, S), F32),
            pltpu.VMEM((SAME, KC, S), F32),
            DMA, DMA, DMA, DMA,
            DMA((NZ - 1,)), DMA((NZ - 1,)), DMA((NZ,)), DMA((NZ,)),
        ],
        compiler_params=pltpu.CompilerParams(
            collective_id=1, has_side_effects=True, vmem_limit_bytes=VMEM_BYTES
        ),
        name="scatter",
    )(part_mon, part_out)
    grad_mon, grad_out = pl.pallas_call(
        store_kernel,
        out_shape=(
            jax.ShapeDtypeStruct((OWN, S), F32),
            jax.ShapeDtypeStruct((SAME * KC, S), F32),
        ),
        in_specs=vmem(2),
        out_specs=tuple([pl.BlockSpec(memory_space=pltpu.HBM)] * 2),
        scratch_shapes=[DMA((2,))],
        compiler_params=pltpu.CompilerParams(vmem_limit_bytes=VMEM_BYTES),
        name="store",
    )(grad_mon, grad_out)
    return grad_mon, grad_out[None]


def solution(mesh):
    in_specs = (
        P("mon", None),
        P("out", "mon", None),
        P("mon"),
        P(),
        P("mon", "out", None, None, None),
        P("mon", "out", None),
        P("mon", "out", None),
        P("mon", "out"),
    )
    out_specs = (P(("mon", "out"), None), P("out", "mon", None))
    return jax.shard_map(local, mesh=mesh, in_specs=in_specs, out_specs=out_specs, check_vma=False)
```
